32 devices in a mesh: wide: 8 (over z, x), narrow: 4 (over y, core).
Axes of the slice: x: 2, y: 2, z: 4, core: 2. Of those that a mesh axis runs over, the one named last changes fastest.
Arguments:
- tokens: bfloat16 [4096, 2048], P(('wide', 'narrow')), may hold values from -6 to 6
- expert_ids: int32 [4096], P(('wide', 'narrow')), may hold values from 0 to 3, as said below
- route_weights: float32 [4096], P(('wide', 'narrow')), may hold values from 0.2 to 1
- out_grad: bfloat16 [4096, 2048], P(('wide', 'narrow')), may hold values from -0.796875 to 0.796875
- w_gate_up: bfloat16 [32, 2048, 256], P(('wide', 'narrow')), may hold values from -0.125 to 0.125
- w_down: bfloat16 [32, 128, 2048], P(('wide', 'narrow')), may hold values from -0.375 to 0.375
- second_moment: bfloat16 [32, 128, 2048], P(('wide', 'narrow')), may hold values from 0.0049743652 to 0.099609375
Outputs:
- grad_gate_up: bfloat16 [32, 2048, 256], P(('wide', 'narrow'))
- down_update: bfloat16 [32, 128, 2048], P(('wide', 'narrow'))
The draws below stay inside these ranges and needn't reach their ends.
Inputs may be any that keep to these rules, and one draw needn't show every extreme that they name: `expert_ids`: values below 2 name the token's own group's experts, the others the next group's. Within the rows of one device no value appears more than 48 times; in every group of 4 devices along narrow one value appears exactly 48 times on every device of the group.
All inputs are finite; a program needn't handle non-finite values.
Results may differ from the reference program's by a relative error of at most 0.0066.
Values may be sent and summed in bfloat16 or wider, within the bound.
A program may use at most 64 MiB of HBM per device.

```python
import math
import jax
import jax.numpy as jnp
from jax import lax

D = 2048
FF = 256
TOK_DEV = 128
HALF = 128
CAP = 48
TOKENS = 4096
SLABS = 32
N_WIDE = 8
N_NARROW = 4


def draw_expert_ids(key, part):
    groups = N_NARROW
    others = groups - 1
    remaining = TOK_DEV - CAP
    base_count = remaining // others
    extra_count = remaining - base_count * others
    pair_count = others // 2
    spread = max(0, min(base_count, CAP - base_count - 1))

    def one_device(device):
        group_key = jax.random.fold_in(jax.random.fold_in(key, 11), device // groups)
        full_expert = jax.random.randint(group_key, (), 0, groups)
        device_key = jax.random.fold_in(jax.random.fold_in(key, 23), device)
        order_key, shift_key, place_key = jax.random.split(device_key, 3)
        shuffle = jax.random.permutation(order_key, others)
        shifts = jax.random.randint(shift_key, (pair_count,), 0, spread + 1)
        signed = jnp.stack([shifts, -shifts], axis=1).reshape(-1)
        signed = jnp.concatenate([signed, jnp.zeros((others - 2 * pair_count,), jnp.int32)])
        counts = base_count + (jnp.arange(others) < extra_count).astype(jnp.int32) + signed
        owners = (full_expert + 1 + shuffle) % groups
        totals = jnp.zeros((groups,), jnp.int32).at[owners].set(counts).at[full_expert].set(CAP)
        bounds = jnp.cumsum(totals)
        positions = jnp.arange(TOK_DEV)
        labels = jnp.sum((positions[:, None] >= bounds[None, :]).astype(jnp.int32), axis=1)
        return labels[jax.random.permutation(place_key, TOK_DEV)]
    return jax.vmap(one_device)(jnp.arange(TOKENS // TOK_DEV)).reshape(-1).astype(jnp.int32)


def level_of(rng, dims, cuts, smallest, largest):
    def one(dim, blocks):
        steps = jax.random.uniform(jax.random.fold_in(jax.random.fold_in(rng, 6), dim), (blocks,), jnp.float32, smallest / len(cuts), largest / len(cuts))
        return jnp.repeat(jnp.exp(steps), dims[dim] // blocks).reshape((-1,) + (1,) * (len(dims) - dim - 1))

    loudness = one(*cuts[0])
    for cut in cuts[1:]:
        loudness = loudness * one(*cut)
    return loudness


def bell_draw(own_key, dims, width, most, cuts=(), kind=jnp.bfloat16):
    factor_of = level_of(own_key, dims, cuts, -0.22, 0.18) if cuts else 1.0
    drawn = jax.random.normal(own_key, dims, jnp.float32) * width * factor_of
    return jnp.minimum(jnp.maximum(drawn, -most), most).astype(kind)


def setup_inputs(seed: int = 0) -> dict:
    key_list = jax.random.split(jax.random.key(seed), 8)
    return {
        "tokens": bell_draw(key_list[0], (TOKENS, D), 1.0, 6.0, ((0, 32),)),
        "expert_ids": draw_expert_ids(jax.random.fold_in(key_list[7], 71), 0),
        "route_weights": jnp.clip(0.2 + 0.8 * jax.random.uniform(key_list[2], (TOKENS,), jnp.float32) ** level_of(key_list[2], (TOKENS,), ((0, 32),), -0.2, 0.2), 0.2, 1.0),
        "out_grad": bell_draw(key_list[3], (TOKENS, D), 0.1, 0.796875, ((0, 32),)),
        "w_gate_up": bell_draw(key_list[4], (SLABS, D, FF), D ** -0.5, 0.125, ((0, 32),)),
        "w_down": bell_draw(key_list[5], (SLABS, HALF, D), FF ** -0.5, 0.375, ((0, 32),)),
        "second_moment": jnp.clip(jnp.exp(math.log(0.099609375) - 2.9969585 * jax.random.uniform(key_list[6], (SLABS, HALF, D), jnp.float32) ** level_of(key_list[6], (SLABS, HALF, D), ((0, 32),), -0.2, 0.2)), 0.0049743652, 0.099609375).astype(jnp.bfloat16),
    }


second_correction = 1.0 - 0.95 ** 10

def term_grads(rows_x, rows_d, weight_gu, weight_dn):
    width_half = weight_dn.shape[0]
    projected = jnp.dot(rows_x, weight_gu, preferred_element_type=jnp.float32)
    gate_pre = projected[:, :width_half]
    up_pre = projected[:, width_half:]
    logistic = jax.nn.sigmoid(gate_pre)
    swished = gate_pre * logistic
    hidden = (swished * up_pre).astype(jnp.bfloat16)
    down_grad = jnp.dot(hidden.T, rows_d, preferred_element_type=jnp.float32)
    hidden_grad = jnp.dot(rows_d, weight_dn.T, preferred_element_type=jnp.float32)
    gate_grad = hidden_grad * up_pre * logistic * (1.0 + gate_pre * (1.0 - logistic))
    up_grad = hidden_grad * swished
    pre_grads = jnp.concatenate([gate_grad, up_grad], axis=1).astype(jnp.bfloat16)
    proj_grad = jnp.dot(rows_x.T, pre_grads, preferred_element_type=jnp.float32)
    return (proj_grad, down_grad)

def dispatch_rows(rows, labels):
    experts_axis = jnp.arange(N_NARROW, dtype=jnp.int32)
    onehot = (labels[:, None] == experts_axis[None, :]).astype(jnp.int32)
    within = lax.optimization_barrier(jnp.sum((jnp.cumsum(onehot, axis=0) - onehot) * onehot, axis=1))
    target = labels * CAP + within
    columns = jnp.arange(N_NARROW * CAP, dtype=jnp.int32)
    select = (target[:, None] == columns[None, :]).astype(rows.dtype)
    placed = jnp.dot(select.T, rows, preferred_element_type=jnp.float32).astype(rows.dtype)
    return placed.reshape(N_NARROW, CAP, D)

def reference(tokens, expert_ids, route_weights, out_grad, w_gate_up, w_down, second_moment):
    devices = N_WIDE * N_NARROW
    half_groups = N_NARROW // 2
    scaled = (route_weights[:, None] * out_grad.astype(jnp.float32)).astype(jnp.bfloat16)
    labels = expert_ids.reshape(devices, TOK_DEV)
    row_buffers = jax.vmap(dispatch_rows)(tokens.reshape(devices, TOK_DEV, D), labels)
    grad_buffers = jax.vmap(dispatch_rows)(scaled.reshape(devices, TOK_DEV, D), labels)
    row_buffers = row_buffers.reshape(N_WIDE, N_NARROW, N_NARROW, CAP, D)
    grad_buffers = grad_buffers.reshape(N_WIDE, N_NARROW, N_NARROW, CAP, D)

    def per_slab(slab_index):
        wide_index = slab_index // N_NARROW
        narrow_index = slab_index % N_NARROW
        previous = (wide_index + N_WIDE - 1) % N_WIDE
        local_expert = narrow_index // 2
        own_x = row_buffers[wide_index, :, local_expert].reshape(N_NARROW * CAP, D)
        own_d = grad_buffers[wide_index, :, local_expert].reshape(N_NARROW * CAP, D)
        near_x = row_buffers[previous, :, half_groups + local_expert].reshape(N_NARROW * CAP, D)
        near_d = grad_buffers[previous, :, half_groups + local_expert].reshape(N_NARROW * CAP, D)
        weight_gu = w_gate_up[slab_index]
        weight_dn = w_down[slab_index]
        own_proj, own_down = term_grads(own_x, own_d, weight_gu, weight_dn)
        near_proj, near_down = term_grads(near_x, near_d, weight_gu, weight_dn)
        rounded = lax.optimization_barrier((near_proj.astype(jnp.bfloat16), near_down.astype(jnp.bfloat16)))
        total_proj = own_proj + rounded[0].astype(jnp.float32)
        total_down = own_down + rounded[1].astype(jnp.float32)
        second = 0.95 * second_moment[slab_index].astype(jnp.float32) + 0.05 * total_down * total_down
        update = total_down / (jnp.sqrt(second / second_correction) + 1e-08) + 0.1 * weight_dn.astype(jnp.float32)
        return (total_proj.astype(jnp.bfloat16), update.astype(jnp.bfloat16))
    grad_gate_up, down_update = lax.map(per_slab, jnp.arange(devices, dtype=jnp.int32))
    return (grad_gate_up, down_update)
```

```python
import functools

import jax
import jax.numpy as jnp
from jax import lax
from jax.experimental import pallas as pl
from jax.experimental.pallas import tpu as pltpu
from jax.sharding import PartitionSpec as P

second_correction = 1.0 - 0.95**10
bf16 = jnp.bfloat16
f32 = jnp.float32
LIMIT = 32 * 1024 * 1024


def mm(a, b, dims):
    return lax.dot_general(a, b, (dims, ((), ())), preferred_element_type=f32)


RELAYED = True
LENDS = 2
GATE = 1
PACK = (2, 3, 3)
FIRST_X = (2, 3, 3)
EARLY_D = (5, 3)
DIAGONAL_X = (4, 4)
LATE_D = (2, 2, 2, 1, 1)


def spans(width, weights):
    unit = width // sum(weights)
    out, at = [], 0
    for weight in weights:
        out.append((at * unit, weight * unit))
        at += weight
    return out


def kernel(
    groups, wides, slot, relayed,
    ids_hbm, rw_hbm, tok_hbm, og_hbm, wgu_hbm, wdn_hbm, sm_hbm,
    acc_p, turned, pre_last, ustage,
    ids, rw, tok, og, wgu, wdn, sm, px, pd, rx, rd, lent, pre, hid, acc_d, moment, decay,
    in_sem, send_sem, recv_sem, lent_sem, pass_sem, fsend_sem, frecv_sem, twice_sem, ready_sem,
):
    half = groups // 2
    width = tok.shape[1]
    hidden_units = wdn.shape[0]
    wide = lax.axis_index("wide")
    narrow = lax.axis_index("narrow")
    home = narrow // 2
    parity = lax.rem(narrow, 2)

    def along(step):
        return lax.rem(wide + wides + step, wides)

    def device(w, n):
        return {"wide": w, "narrow": n}

    def peer(j):
        return 2 * lax.rem(home + j, half) + parity

    odd = lax.rem(wide, 2) == 1
    even = jnp.logical_not(odd)
    sibling = device(wide, 2 * home + 1 - parity)

    order = [(0, 0), (1, 0)] + [(0, j) for j in range(2, half)]
    order += [(1, j) for j in range(1, half)] + [(0, 1)]
    early = list(range(half))
    late = list(range(half, groups))
    direct = 1
    diagonal = [b for b in late if order[b][0]]
    beside = [b for b in range(1, groups) if not order[b][0]]

    loads = []
    for i, (src, dst) in enumerate(
        (
            (tok_hbm, tok), (og_hbm, og), (wgu_hbm.at[0], wgu), (wdn_hbm.at[0], wdn),
            (sm_hbm.at[0], sm), (ids_hbm, ids), (rw_hbm, rw),
        )
    ):
        loads.append(pltpu.make_async_copy(src, dst, in_sem.at[i]))
    for i in (5, 0, 6, 1):
        loads[i].start()

    barrier = pltpu.get_barrier_semaphore()

    def signal(sem, partner):
        pl.semaphore_signal(sem, inc=1, device_id=partner, device_id_type=pl.DeviceIdType.MESH)

    signal(barrier, device(along(-1), narrow))
    for j in range(1, half):
        signal(barrier, device(wide, peer(j)))
    signal(barrier, sibling)
    if relayed:

        @pl.when(even)
        def _():
            signal(barrier, device(along(1), narrow))

    loads[5].wait()
    count = tok.shape[0]
    labels = ids[...]
    pad_groups = max(8, groups)
    onehot = (lax.broadcasted_iota(jnp.int32, (pad_groups, count), 0) == labels).astype(f32)
    before = (
        lax.broadcasted_iota(jnp.int32, (count, count), 0)
        < lax.broadcasted_iota(jnp.int32, (count, count), 1)
    ).astype(f32)
    counted = mm(onehot.astype(bf16), before.astype(bf16), ((1,), (0,)))
    within = jnp.sum(counted * onehot, axis=0, keepdims=True).astype(jnp.int32)
    slots = lax.broadcasted_iota(jnp.int32, (slot, count), 0)

    def select_of(b):
        kind, j = order[b]
        value = kind * half + lax.rem(home + j, half)
        return jnp.logical_and(labels == value, slots == within)

    def rows(b, h):
        return pl.ds((2 * b + h) * slot, slot)

    def remote(src, dst, s, r, dev):
        return pltpu.make_async_remote_copy(
            src_ref=src, dst_ref=dst, send_sem=s, recv_sem=r,
            device_id=dev, device_id_type=pl.DeviceIdType.MESH,
        )

    index, parts = {}, {}
    for b in range(1, groups):
        widths = (DIAGONAL_X if b in diagonal else FIRST_X, EARLY_D if b in early else LATE_D)
        for a in (0, 1):
            parts[b, a] = spans(width, widths[a])
            for c in range(len(parts[b, a])):
                index[b, a, c] = len(index)
    packed, received = (px, pd), (rx, rd)

    def cols_of(b, a, c):
        return pl.ds(*parts[b, a][c])

    def send(b, a, c):
        kind, j = order[b]
        cols = cols_of(b, a, c)
        return remote(
            packed[a].at[b - 1, :, cols], received[a].at[rows(b, 0), cols],
            send_sem.at[2 if a == 0 and b == direct and c < lends else a], recv_sem.at[index[b, a, c]], device(along(kind), peer(j)),
        )

    lends = LENDS if relayed else 0

    def lend(c):
        cols = cols_of(direct, 0, c)
        return remote(
            px.at[direct - 1, :, cols], lent.at[:, cols],
            send_sem.at[2], lent_sem.at[c], device(along(-1), narrow),
        )

    def hand_on(c):
        cols = cols_of(direct, 0, c)
        return remote(
            lent.at[:, cols], rx.at[rows(direct, 0), cols],
            pass_sem.at[0], recv_sem.at[index[direct, 0, c]], device(along(2), narrow),
        )

    def go_first(c):
        if relayed:

            @pl.when(odd)
            def _():
                lend(c).start()

            @pl.when(even)
            def _():
                send(direct, 0, c).start()
        else:
            send(direct, 0, c).start()

    def go_rest():
        for c in range(lends, len(FIRST_X)):
            send(direct, 0, c).start()
        for c in range(len(parts[direct, 1])):
            send(direct, 1, c).start()
        for a in (0, 1):
            for b in diagonal:
                for c in range(len(parts[b, a]) - a):
                    send(b, a, c).start()

    def first_sent():
        part = px.at[0, :, pl.ds(0, first_columns)]
        remote(part, part, send_sem.at[2], recv_sem.at[0], sibling).wait_send()

    held_back = jnp.logical_and(odd, wide != wides - 1)
    first_columns = sum(FIRST_X[:lends]) * width // sum(FIRST_X)

    final = len(LATE_D) - 1

    def send_twice(b):
        kind, j = order[b]
        cols, other = cols_of(b, 1, final), 2 * lax.rem(home + j, half) + 1 - parity
        return remote(
            pd.at[b - 1, :, cols], rd.at[rows(b, 1), cols],
            twice_sem.at[0], twice_sem.at[1 + b - half], device(along(kind), other),
        )

    def forward(b, a, c):
        cols = cols_of(b, a, c)
        which = a if b < half else 2 + (b in beside) if a == 0 else 4 + c
        return remote(
            received[a].at[rows(b, 0), cols], received[a].at[rows(b, 1), cols],
            fsend_sem.at[a], frecv_sem.at[which], sibling,
        )

    def settle(which, a, blocks, cols=slice(None)):
        part = received[a].at[pl.ds(0, blocks * slot), cols]
        remote(part, part, fsend_sem.at[a], frecv_sem.at[which], sibling).wait_recv()

    selects = [select_of(b) for b in range(groups)]
    chosen = jnp.concatenate([s.astype(f32) for s in selects], axis=0).astype(bf16)

    def store(a, cols, block):
        for b in range(groups):
            piece = block[b * slot : (b + 1) * slot]
            if b:
                packed[a][b - 1, :, cols] = piece
            else:
                received[a][rows(0, 0), cols] = piece

    loads[0].wait()
    for i in (2, 3, 4):
        loads[i].start()
    for n, (start, size) in enumerate(spans(width, PACK)):
        cols = pl.ds(start, size)
        store(0, cols, mm(chosen, tok[:, cols], ((1,), (0,))).astype(bf16))
        if n == 0:
            near = 1 + half - 1 + 1
            if relayed:

                @pl.when(odd)
                def _():
                    pl.semaphore_wait(barrier, near + 1)

                @pl.when(even)
                def _():
                    pl.semaphore_wait(barrier, near)
            else:
                pl.semaphore_wait(barrier, near)
        for c, (at, extent) in enumerate(spans(width, FIRST_X)):
            if at + extent == start + size:
                if c < lends:
                    go_first(c)
                for b in beside:
                    send(b, 0, c).start()
        if n == 0:
            for j in range(1, half):
                signal(ready_sem, device(wide, peer(j)))
    loads[6].wait()
    weights = rw[...]
    weight = jnp.concatenate(
        [jnp.sum(jnp.where(s, weights, 0.0), axis=1, keepdims=True) for s in selects], axis=0
    )
    loads[1].wait()
    for start, size in spans(width, PACK):
        cols = pl.ds(start, size)
        placed = mm(chosen, og[:, cols], ((1,), (0,)))
        store(1, cols, (weight * placed).astype(bf16))
    for b in beside:
        for c in range(len(parts[b, 1]) - (b in late)):
            send(b, 1, c).start()
    if half > 1:
        pl.semaphore_wait(ready_sem, half - 1)
    if relayed:
        pl.when(jnp.logical_not(held_back))(go_rest)
    else:
        go_rest()
    for a in (0, 1):
        whole = received[a]
        remote(
            whole.at[rows(0, 0)], whole.at[rows(0, 1)],
            fsend_sem.at[a], frecv_sem.at[a], sibling,
        ).start()
    loads[2].wait()
    loads[3].wait()
    loads[4].wait()
    if relayed:

        @pl.when(even)
        def _():
            for c in range(lends):
                lend(c).wait_recv()
                hand_on(c).start()

    def project(r):
        projected = mm(rx[r, :], wgu[...], ((1,), (0,)))
        gate_pre = projected[:, :hidden_units]
        up_pre = projected[:, hidden_units:]
        logistic = jax.nn.sigmoid(gate_pre)
        swished = gate_pre * logistic
        hid[r, :] = (swished * up_pre).astype(bf16)
        return up_pre * logistic * (1.0 + gate_pre * (1.0 - logistic)), swished

    def finish(target, r, hidden_grad, factors):
        target[r, :] = jnp.concatenate(
            [hidden_grad * factors[0], hidden_grad * factors[1]], axis=1
        ).astype(bf16)

    def take(b, a, c):
        send(b, a, c).wait_recv()
        forward(b, a, c).start()

    def take_all(blocks, a):
        for b in blocks:
            for c in range(len(parts[b, a])):
                take(b, a, c)
                if relayed and (b, a, c) == (direct, 0, GATE):
                    pl.when(held_back)(go_rest)

    take_all(early[1:], 0)
    take_all([late[-1]], 0)
    settle(0, 0, half)
    settle(3, 0, 1)
    first = pl.ds(0, half * 2 * slot)
    last = pl.ds(half * 2 * slot, half * 2 * slot)
    factors_first = project(first)
    take_all(early[1:], 1)
    for b in late:
        send(b, 1, final).start()
        send_twice(b).start()
    moment[...] = (0.95 / second_correction) * sm[...].astype(f32)
    decay[...] = 0.1 * wdn[...].astype(f32)
    settle(1, 1, half)
    finish(pre, first, mm(rd[first, :], wdn[...], ((1,), (1,))), factors_first)
    for i in range(width // 256):
        cols = pl.ds(i * 256, 256)
        acc_p[cols, :] = mm(rx[first, cols], pre[first, :], ((0,), (0,)))
        acc_d[:, cols] = mm(hid[first, :], rd[first, cols], ((0,), (0,)))
    take_all(diagonal, 0)
    settle(2, 0, half - 1)
    factors = project(last)
    turned[...] = rx[last, :].T
    turned_hid = hid[last, :].T
    hidden_grad = jnp.zeros((half * 2 * slot, hidden_units), f32)
    late_d = spans(width, LATE_D)

    def relay(c):
        for b in late:
            take(b, 1, c)

    def add(c):
        cols = pl.ds(*late_d[c])
        return hidden_grad + mm(rd[last, cols], wdn[:, cols], ((1,), (1,)))

    def update(c):
        cols = pl.ds(*late_d[c])
        total = acc_d[:, cols] + mm(turned_hid, rd[last, cols], ((1,), (0,)))
        second = moment[:, cols] + (0.05 / second_correction) * total * total
        root = second * lax.rsqrt(second)
        ustage[:, cols] = (total / (root + 1e-08) + decay[:, cols]).astype(bf16)

    for c in range(final):
        relay(c)
    for c in range(final):
        settle(4 + c, 1, half, pl.ds(*late_d[c]))
        hidden_grad = add(c)
        update(c)
    for b in late:
        send(b, 1, final).wait_recv()
        send_twice(b).wait_recv()
    hidden_grad = add(final)
    finish(pre_last, slice(None), hidden_grad, factors)
    update(final)
    part = px.at[1:]
    remote(part, part, send_sem.at[0], recv_sem.at[0], sibling).wait_send()
    if relayed:
        first_sent()
        part = px.at[0, :, pl.ds(first_columns, width - first_columns)]
        remote(part, part, send_sem.at[0], recv_sem.at[0], sibling).wait_send()
    else:
        remote(px.at[0], px.at[0], send_sem.at[0], recv_sem.at[0], sibling).wait_send()
    remote(pd, pd, send_sem.at[1], recv_sem.at[0], sibling).wait_send()
    part = rx.at[pl.ds(0, groups * slot)]
    remote(part, part, fsend_sem.at[0], frecv_sem.at[0], sibling).wait_send()
    part, cols = rd.at[pl.ds(0, groups * slot)], pl.ds(0, late_d[final][0])
    rest = pl.ds(late_d[final][0], late_d[final][1])
    remote(part.at[:, cols], part.at[:, cols], fsend_sem.at[1], frecv_sem.at[0], sibling).wait_send()
    part = rd.at[pl.ds(0, half * slot), rest]
    remote(part, part, fsend_sem.at[1], frecv_sem.at[0], sibling).wait_send()
    remote(part, part, twice_sem.at[0], frecv_sem.at[0], sibling).wait_send()
    if relayed:

        @pl.when(even)
        def _():
            part = lent.at[:, pl.ds(0, first_columns)]
            remote(part, part, pass_sem.at[0], recv_sem.at[0], sibling).wait_send()


def final_kernel(acc_p, turned, pre_last, update, gout, uout, gstage, out_sem):
    tiles = acc_p.shape[0] // 256
    outs = [pltpu.make_async_copy(update, uout.at[0], out_sem.at[tiles])]
    outs[0].start()
    for i in range(tiles):
        r = pl.ds(i * 256, 256)
        gstage[r, :] = (acc_p[r, :] + mm(turned[r, :], pre_last[...], ((1,), (0,)))).astype(bf16)
        copy = pltpu.make_async_copy(gstage.at[r], gout.at[0, r], out_sem.at[i])
        copy.start()
        outs.append(copy)
    for copy in outs:
        copy.wait()


def body(tokens, expert_ids, route_weights, out_grad, w_gate_up, w_down, second_moment):
    groups = lax.axis_size("narrow")
    wides = lax.axis_size("wide")
    count, width = tokens.shape
    cap = 3 * count // (2 * groups)
    slot = -(-cap // 16) * 16
    columns = w_gate_up.shape[2]
    units = w_down.shape[1]
    half = groups // 2
    all_rows = groups * 2 * slot
    last_rows = half * 2 * slot
    relayed = RELAYED and wides % 2 == 0 and wides >= 4
    chunks = (groups - 1) * (len(FIRST_X) + len(LATE_D))
    dma = pltpu.SemaphoreType.DMA
    any_spec = pl.BlockSpec(memory_space=pl.ANY)
    vmem_spec = pl.BlockSpec(memory_space=pltpu.VMEM)
    held = pl.pallas_call(
        functools.partial(kernel, groups, wides, slot, relayed),
        out_shape=(
            pltpu.VMEM((width, columns), f32),
            pltpu.VMEM((width, last_rows), bf16),
            pltpu.VMEM((last_rows, columns), bf16),
            pltpu.VMEM((units, width), bf16),
        ),
        in_specs=[any_spec] * 7,
        out_specs=(vmem_spec,) * 4,
        scratch_shapes=[
            pltpu.VMEM((1, count), jnp.int32),
            pltpu.VMEM((1, count), f32),
            pltpu.VMEM((count, width), bf16),
            pltpu.VMEM((count, width), bf16),
            pltpu.VMEM((width, columns), bf16),
            pltpu.VMEM((units, width), bf16),
            pltpu.VMEM((units, width), bf16),
            pltpu.VMEM((groups - 1, slot, width), bf16),
            pltpu.VMEM((groups - 1, slot, width), bf16),
            pltpu.VMEM((all_rows, width), bf16),
            pltpu.VMEM((all_rows, width), bf16),
            pltpu.VMEM((slot, width), bf16),
            pltpu.VMEM((last_rows, columns), bf16),
            pltpu.VMEM((all_rows, units), bf16),
            pltpu.VMEM((units, width), f32),
            pltpu.VMEM((units, width), f32),
            pltpu.VMEM((units, width), f32),
            dma((7,)), dma((3,)), dma((chunks,)), dma((len(FIRST_X),)), dma((1,)), dma((2,)),
            dma((4 + len(LATE_D),)), dma((1 + half,)), pltpu.SemaphoreType.REGULAR,
        ],
        compiler_params=pltpu.CompilerParams(
            collective_id=0, has_side_effects=True, vmem_limit_bytes=LIMIT
        ),
    )(
        *(
            pltpu.with_memory_space_constraint(value, pltpu.HBM)
            for value in (
                expert_ids.reshape(1, count), route_weights.reshape(1, count),
                tokens, out_grad, w_gate_up, w_down, second_moment,
            )
        ),
    )
    return pl.pallas_call(
        final_kernel,
        out_shape=(
            jax.ShapeDtypeStruct((1, width, columns), bf16),
            jax.ShapeDtypeStruct((1, units, width), bf16),
        ),
        in_specs=[vmem_spec] * 4,
        out_specs=(any_spec, any_spec),
        scratch_shapes=[pltpu.VMEM((width, columns), bf16), dma((width // 256 + 1,))],
        compiler_params=pltpu.CompilerParams(vmem_limit_bytes=LIMIT),
    )(*held)


def solution(mesh):
    placed = (
        P(("wide", "narrow"), None),
        P(("wide", "narrow")),
        P(("wide", "narrow")),
        P(("wide", "narrow"), None),
        P(("wide", "narrow"), None, None),
        P(("wide", "narrow"), None, None),
        P(("wide", "narrow"), None, None),
    )
    return jax.shard_map(
        body,
        mesh=mesh,
        in_specs=placed,
        out_specs=(P(("wide", "narrow"), None, None), P(("wide", "narrow"), None, None)),
        check_vma=False,
    )
```

```python
import functools

import jax
import jax.numpy as jnp
from jax import lax
from jax.experimental import pallas as pl
from jax.experimental.pallas import tpu as pltpu
from jax.sharding import PartitionSpec as P

second_correction = 1.0 - 0.95**10
bf16 = jnp.bfloat16
f32 = jnp.float32
LIMIT = 32 * 1024 * 1024


def mm(a, b, dims):
    return lax.dot_general(a, b, (dims, ((), ())), preferred_element_type=f32)


RELAYED = True
LENDS = 2
GATE = 1
PACK = (2, 3, 3)
FIRST_X = (2, 3, 3)
EARLY_D = (5, 3)
DIAGONAL_X = (4, 4)
LATE_D = (2, 2, 2, 1, 1)


def spans(width, weights):
    unit = width // sum(weights)
    out, at = [], 0
    for weight in weights:
        out.append((at * unit, weight * unit))
        at += weight
    return out


def kernel(
    groups, wides, slot, relayed,
    ids_hbm, rw_hbm, tok_hbm, og_hbm, wgu_hbm, wdn_hbm, sm_hbm,
    acc_p, turned, pre_last, ustage,
    ids, rw, tok, og, wgu, wdn, sm, px, pd, rx, rd, lent, pre, hid, acc_d, moment, decay, turned_wdn,
    in_sem, send_sem, recv_sem, lent_sem, pass_sem, fsend_sem, frecv_sem, twice_sem, ready_sem,
):
    half = groups // 2
    width = tok.shape[1]
    hidden_units = wdn.shape[0]
    wide = lax.axis_index("wide")
    narrow = lax.axis_index("narrow")
    home = narrow // 2
    parity = lax.rem(narrow, 2)

    def along(step):
        return lax.rem(wide + wides + step, wides)

    def device(w, n):
        return {"wide": w, "narrow": n}

    def peer(j):
        return 2 * lax.rem(home + j, half) + parity

    odd = lax.rem(wide, 2) == 1
    even = jnp.logical_not(odd)
    sibling = device(wide, 2 * home + 1 - parity)

    order = [(0, 0), (1, 0)] + [(0, j) for j in range(2, half)]
    order += [(1, j) for j in range(1, half)] + [(0, 1)]
    early = list(range(half))
    late = list(range(half, groups))
    direct = 1
    diagonal = [b for b in late if order[b][0]]
    beside = [b for b in range(1, groups) if not order[b][0]]

    loads = []
    for i, (src, dst) in enumerate(
        (
            (tok_hbm, tok), (og_hbm, og), (wgu_hbm.at[0], wgu), (wdn_hbm.at[0], wdn),
            (sm_hbm.at[0], sm), (ids_hbm, ids), (rw_hbm, rw),
        )
    ):
        loads.append(pltpu.make_async_copy(src, dst, in_sem.at[i]))
    for i in (5, 0, 6, 1):
        loads[i].start()

    barrier = pltpu.get_barrier_semaphore()

    def signal(sem, partner):
        pl.semaphore_signal(sem, inc=1, device_id=partner, device_id_type=pl.DeviceIdType.MESH)

    signal(barrier, device(along(-1), narrow))
    for j in range(1, half):
        signal(barrier, device(wide, peer(j)))
    signal(barrier, sibling)
    if relayed:

        @pl.when(even)
        def _():
            signal(barrier, device(along(1), narrow))

    loads[5].wait()
    count = tok.shape[0]
    labels = ids[...]
    pad_groups = max(8, groups)
    onehot = (lax.broadcasted_iota(jnp.int32, (pad_groups, count), 0) == labels).astype(f32)
    before = (
        lax.broadcasted_iota(jnp.int32, (count, count), 0)
        < lax.broadcasted_iota(jnp.int32, (count, count), 1)
    ).astype(f32)
    counted = mm(onehot.astype(bf16), before.astype(bf16), ((1,), (0,)))
    within = jnp.sum(counted * onehot, axis=0, keepdims=True).astype(jnp.int32)
    slots = lax.broadcasted_iota(jnp.int32, (slot, count), 0)

    def select_of(b):
        kind, j = order[b]
        value = kind * half + lax.rem(home + j, half)
        return jnp.logical_and(labels == value, slots == within)

    near = late[-1]
    far = jnp.logical_and(wide == wides - 1, home > 0)
    swapped = jnp.logical_and(wide == 0, home > 0)
    near_swapped = jnp.logical_and(wide == 0, lax.rem(home + 1, half) > 0)
    lent_swapped = jnp.logical_and(along(2) == 0, home > 0)

    def rows(b, h, swap=None):
        if swap is None or b not in (direct, near):
            return pl.ds((2 * b + h) * slot, slot)
        at = jnp.where(swap, direct + near - b, b)
        return pl.ds(pl.multiple_of((2 * at + h) * slot, slot), slot)

    def remote(src, dst, s, r, dev):
        return pltpu.make_async_remote_copy(
            src_ref=src, dst_ref=dst, send_sem=s, recv_sem=r,
            device_id=dev, device_id_type=pl.DeviceIdType.MESH,
        )

    index, parts = {}, {}
    for b in range(1, groups):
        widths = (DIAGONAL_X if b in diagonal else FIRST_X, EARLY_D if b in early[2:] else LATE_D)
        for a in (0, 1):
            parts[b, a] = spans(width, widths[a])
            for c in range(len(parts[b, a])):
                index[b, a, c] = len(index)
    packed, received = (px, pd), (rx, rd)

    def cols_of(b, a, c):
        return pl.ds(*parts[b, a][c])

    def send(b, a, c):
        kind, j = order[b]
        cols = cols_of(b, a, c)
        return remote(
            packed[a].at[b - 1, :, cols],
            received[a].at[rows(b, 0, far if b == direct else near_swapped), cols],
            send_sem.at[2 if a == 0 and b == direct and c < lends else a], recv_sem.at[index[b, a, c]], device(along(kind), peer(j)),
        )

    lends = LENDS if relayed else 0

    def lend(c):
        cols = cols_of(direct, 0, c)
        return remote(
            px.at[direct - 1, :, cols], lent.at[:, cols],
            send_sem.at[2], lent_sem.at[c], device(along(-1), narrow),
        )

    def hand_on(c):
        cols = cols_of(direct, 0, c)
        return remote(
            lent.at[:, cols], rx.at[rows(direct, 0, lent_swapped), cols],
            pass_sem.at[0], recv_sem.at[index[direct, 0, c]], device(along(2), narrow),
        )

    def go_first(c):
        if relayed:

            @pl.when(odd)
            def _():
                lend(c).start()

            @pl.when(even)
            def _():
                send(direct, 0, c).start()
        else:
            send(direct, 0, c).start()

    def go_direct():
        for c in range(len(parts[direct, 1])):
            send(direct, 1, c).start()

    def go_rest():
        for c in range(lends, len(FIRST_X)):
            send(direct, 0, c).start()
        pl.when(jnp.logical_not(far))(go_direct)
        for a in (0, 1):
            for b in diagonal:
                for c in range(len(parts[b, a]) - a):
                    send(b, a, c).start()

    def first_sent():
        part = px.at[0, :, pl.ds(0, first_columns)]
        remote(part, part, send_sem.at[2], recv_sem.at[0], sibling).wait_send()

    held_back = jnp.logical_and(odd, wide != wides - 1)
    first_columns = sum(FIRST_X[:lends]) * width // sum(FIRST_X)

    final = len(LATE_D) - 1

    def send_twice(b):
        kind, j = order[b]
        cols, other = cols_of(b, 1, final), 2 * lax.rem(home + j, half) + 1 - parity
        return remote(
            pd.at[b - 1, :, cols], rd.at[rows(b, 1, near_swapped), cols],
            twice_sem.at[0], twice_sem.at[1 + b - half], device(along(kind), other),
        )

    def forward(b, a, c, late_one):
        cols = cols_of(b, a, c)
        x_sem = 0 if b < half else 2 + (b in beside)
        which = (4 + c if late_one else 1) if a else x_sem
        return remote(
            received[a].at[rows(b, 0, swapped), cols], received[a].at[rows(b, 1, swapped), cols],
            fsend_sem.at[a], frecv_sem.at[which], sibling,
        )

    def settle(which, a, blocks, cols=slice(None)):
        part = received[a].at[pl.ds(0, blocks * slot), cols]
        remote(part, part, fsend_sem.at[a], frecv_sem.at[which], sibling).wait_recv()

    selects = [select_of(b) for b in range(groups)]
    chosen = jnp.concatenate([s.astype(f32) for s in selects], axis=0).astype(bf16)

    def store(a, cols, block):
        for b in range(groups):
            piece = block[b * slot : (b + 1) * slot]
            if b:
                packed[a][b - 1, :, cols] = piece
            else:
                received[a][rows(0, 0), cols] = piece

    loads[0].wait()
    for i in (2, 3, 4):
        loads[i].start()
    for n, (start, size) in enumerate(spans(width, PACK)):
        cols = pl.ds(start, size)
        store(0, cols, mm(chosen, tok[:, cols], ((1,), (0,))).astype(bf16))
        if n == 0:
            near = 1 + half - 1 + 1
            if relayed:

                @pl.when(odd)
                def _():
                    pl.semaphore_wait(barrier, near + 1)

                @pl.when(even)
                def _():
                    pl.semaphore_wait(barrier, near)
            else:
                pl.semaphore_wait(barrier, near)
        for c, (at, extent) in enumerate(spans(width, FIRST_X)):
            if at + extent == start + size:
                if c < lends:
                    go_first(c)
                for b in beside:
                    send(b, 0, c).start()
        if n == 0:
            for j in range(1, half):
                signal(ready_sem, device(wide, peer(j)))
    loads[6].wait()
    weights = rw[...]
    weight = jnp.concatenate(
        [jnp.sum(jnp.where(s, weights, 0.0), axis=1, keepdims=True) for s in selects], axis=0
    )
    loads[1].wait()
    for start, size in spans(width, PACK):
        cols = pl.ds(start, size)
        placed = mm(chosen, og[:, cols], ((1,), (0,)))
        store(1, cols, (weight * placed).astype(bf16))
    for b in beside:
        for c in range(len(parts[b, 1]) - (b in late)):
            send(b, 1, c).start()
    pl.when(near_swapped)(send(near, 1, final).start)
    if half > 1:
        pl.semaphore_wait(ready_sem, half - 1)
    if relayed:
        pl.when(jnp.logical_not(held_back))(go_rest)
    else:
        go_rest()
    for a in (0, 1):
        whole = received[a]
        remote(
            whole.at[rows(0, 0)], whole.at[rows(0, 1)],
            fsend_sem.at[a], frecv_sem.at[a], sibling,
        ).start()
    loads[2].wait()
    loads[3].wait()
    loads[4].wait()
    if relayed:

        @pl.when(even)
        def _():
            for c in range(lends):
                lend(c).wait_recv()
                hand_on(c).start()

    def project(r):
        projected = mm(rx[r, :], wgu[...], ((1,), (0,)))
        gate_pre = projected[:, :hidden_units]
        up_pre = projected[:, hidden_units:]
        logistic = jax.nn.sigmoid(gate_pre)
        swished = gate_pre * logistic
        hid[r, :] = (swished * up_pre).astype(bf16)
        return up_pre * logistic * (1.0 + gate_pre * (1.0 - logistic)), swished

    def finish(target, r, hidden_grad, factors):
        target[r, :] = jnp.concatenate(
            [hidden_grad * factors[0], hidden_grad * factors[1]], axis=1
        ).astype(bf16)

    def take(b, a, c, late_one):
        send(b, a, c).wait_recv()
        forward(b, a, c, late_one).start()

    def take_all(blocks, a):
        for b in blocks:
            for c in range(len(parts[b, a])):
                take(b, a, c, False)
                if relayed and (b, a, c) == (direct, 0, GATE):
                    pl.when(held_back)(go_rest)

    take_all(early[1:], 0)
    take_all([late[-1]], 0)
    settle(0, 0, half)
    settle(3, 0, 1)

    def go_final(b):
        send(b, 1, final).start()
        send_twice(b).start()

    for b in diagonal:
        go_final(b)

    @pl.when(jnp.logical_not(near_swapped))
    def _():
        go_final(near)

    pl.when(far)(go_direct)
    first = pl.ds(0, half * 2 * slot)
    last = pl.ds(half * 2 * slot, half * 2 * slot)
    factors_first = project(first)
    take_all(early[2:], 1)
    rest = pl.ds(*parts[near, 1][final])

    @pl.when(jnp.logical_not(swapped))
    def _():
        take_all([direct], 1)

    @pl.when(swapped)
    def _():
        take_all([near], 1)

    moment[...] = (0.95 / second_correction) * sm[...].astype(f32)
    decay[...] = 0.1 * wdn[...].astype(f32)
    turned_wdn[...] = wdn[...].T
    settle(1, 1, half)
    finish(pre, first, mm(rd[first, :], wdn[...], ((1,), (1,))), factors_first)
    for i in range(width // 256):
        cols = pl.ds(i * 256, 256)
        acc_p[cols, :] = mm(rx[first, cols], pre[first, :], ((0,), (0,)))
        acc_d[:, cols] = mm(hid[first, :], rd[first, cols], ((0,), (0,)))
    take_all(diagonal, 0)

    def relay(c):
        for b in diagonal:
            take(b, 1, c, True)

        @pl.when(jnp.logical_not(swapped))
        def _():
            take(near, 1, c, True)

        @pl.when(swapped)
        def _():
            take(direct, 1, c, True)

    @pl.when(parity == 1)
    def _():
        for c in range(final):
            relay(c)

    settle(2, 0, half - 1)
    factors = project(last)
    turned[...] = rx[last, :].T
    turned_hid = hid[last, :].T
    hidden_grad = jnp.zeros((half * 2 * slot, hidden_units), f32)
    late_d = spans(width, LATE_D)

    def add(c):
        cols = pl.ds(*late_d[c])
        return hidden_grad + mm(rd[last, cols], turned_wdn[cols, :], ((1,), (0,)))

    def update(c):
        cols = pl.ds(*late_d[c])
        total = acc_d[:, cols] + mm(turned_hid, rd[last, cols], ((1,), (0,)))
        second = moment[:, cols] + (0.05 / second_correction) * total * total
        root = second * lax.rsqrt(second)
        ustage[:, cols] = (total / (root + 1e-08) + decay[:, cols]).astype(bf16)

    for c in range(final):

        @pl.when(parity == 0)
        def _():
            relay(c)

        settle(4 + c, 1, half, pl.ds(*late_d[c]))
        hidden_grad = add(c)
        update(c)
    for b in diagonal:
        send(b, 1, final).wait_recv()
        send_twice(b).wait_recv()

    @pl.when(jnp.logical_not(swapped))
    def _():
        send(near, 1, final).wait_recv()
        send_twice(near).wait_recv()

    @pl.when(swapped)
    def _():
        take(direct, 1, final, True)
        settle(4 + final, 1, 1, rest)

    hidden_grad = add(final)
    finish(pre_last, slice(None), hidden_grad, factors)
    update(final)
    part = px.at[1:]
    remote(part, part, send_sem.at[0], recv_sem.at[0], sibling).wait_send()
    if relayed:
        first_sent()
        part = px.at[0, :, pl.ds(first_columns, width - first_columns)]
        remote(part, part, send_sem.at[0], recv_sem.at[0], sibling).wait_send()
    else:
        remote(px.at[0], px.at[0], send_sem.at[0], recv_sem.at[0], sibling).wait_send()
    remote(pd, pd, send_sem.at[1], recv_sem.at[0], sibling).wait_send()
    part = rx.at[pl.ds(0, groups * slot)]
    remote(part, part, fsend_sem.at[0], frecv_sem.at[0], sibling).wait_send()
    part, cols = rd.at[pl.ds(0, groups * slot)], pl.ds(0, late_d[final][0])
    remote(part.at[:, cols], part.at[:, cols], fsend_sem.at[1], frecv_sem.at[0], sibling).wait_send()
    part = rd.at[pl.ds(0, half * slot), rest]
    remote(part, part, fsend_sem.at[1], frecv_sem.at[0], sibling).wait_send()
    part = rd.at[pl.ds(0, slot), rest]

    @pl.when(jnp.logical_not(near_swapped))
    def _():
        remote(part, part, twice_sem.at[0], frecv_sem.at[0], sibling).wait_send()

    @pl.when(swapped)
    def _():
        remote(part, part, fsend_sem.at[1], frecv_sem.at[0], sibling).wait_send()

    for _ in diagonal:
        remote(part, part, twice_sem.at[0], frecv_sem.at[0], sibling).wait_send()
    if relayed:

        @pl.when(even)
        def _():
            part = lent.at[:, pl.ds(0, first_columns)]
            remote(part, part, pass_sem.at[0], recv_sem.at[0], sibling).wait_send()


def final_kernel(acc_p, turned, pre_last, update, gout, uout, gstage, out_sem):
    tiles = acc_p.shape[0] // 256
    outs = [pltpu.make_async_copy(update, uout.at[0], out_sem.at[tiles])]
    outs[0].start()
    for i in range(tiles):
        r = pl.ds(i * 256, 256)
        gstage[r, :] = (acc_p[r, :] + mm(turned[r, :], pre_last[...], ((1,), (0,)))).astype(bf16)
        copy = pltpu.make_async_copy(gstage.at[r], gout.at[0, r], out_sem.at[i])
        copy.start()
        outs.append(copy)
    for copy in outs:
        copy.wait()


def body(tokens, expert_ids, route_weights, out_grad, w_gate_up, w_down, second_moment):
    groups = lax.axis_size("narrow")
    wides = lax.axis_size("wide")
    count, width = tokens.shape
    cap = 3 * count // (2 * groups)
    slot = -(-cap // 16) * 16
    columns = w_gate_up.shape[2]
    units = w_down.shape[1]
    half = groups // 2
    all_rows = groups * 2 * slot
    last_rows = half * 2 * slot
    relayed = RELAYED and wides % 2 == 0 and wides >= 4
    chunks = (groups - 1) * (len(FIRST_X) + len(LATE_D))
    dma = pltpu.SemaphoreType.DMA
    any_spec = pl.BlockSpec(memory_space=pl.ANY)
    vmem_spec = pl.BlockSpec(memory_space=pltpu.VMEM)
    held = pl.pallas_call(
        functools.partial(kernel, groups, wides, slot, relayed),
        out_shape=(
            pltpu.VMEM((width, columns), f32),
            pltpu.VMEM((width, last_rows), bf16),
            pltpu.VMEM((last_rows, columns), bf16),
            pltpu.VMEM((units, width), bf16),
        ),
        in_specs=[any_spec] * 7,
        out_specs=(vmem_spec,) * 4,
        scratch_shapes=[
            pltpu.VMEM((1, count), jnp.int32),
            pltpu.VMEM((1, count), f32),
            pltpu.VMEM((count, width), bf16),
            pltpu.VMEM((count, width), bf16),
            pltpu.VMEM((width, columns), bf16),
            pltpu.VMEM((units, width), bf16),
            pltpu.VMEM((units, width), bf16),
            pltpu.VMEM((groups - 1, slot, width), bf16),
            pltpu.VMEM((groups - 1, slot, width), bf16),
            pltpu.VMEM((all_rows, width), bf16),
            pltpu.VMEM((all_rows, width), bf16),
            pltpu.VMEM((slot, width), bf16),
            pltpu.VMEM((last_rows, columns), bf16),
            pltpu.VMEM((all_rows, units), bf16),
            pltpu.VMEM((units, width), f32),
            pltpu.VMEM((units, width), f32),
            pltpu.VMEM((units, width), f32),
            pltpu.VMEM((width, units), bf16),
            dma((7,)), dma((3,)), dma((chunks,)), dma((len(FIRST_X),)), dma((1,)), dma((2,)),
            dma((4 + len(LATE_D),)), dma((1 + half,)), pltpu.SemaphoreType.REGULAR,
        ],
        compiler_params=pltpu.CompilerParams(
            collective_id=0, has_side_effects=True, vmem_limit_bytes=LIMIT
        ),
    )(
        *(
            pltpu.with_memory_space_constraint(value, pltpu.HBM)
            for value in (
                expert_ids.reshape(1, count), route_weights.reshape(1, count),
                tokens, out_grad, w_gate_up, w_down, second_moment,
            )
        ),
    )
    return pl.pallas_call(
        final_kernel,
        out_shape=(
            jax.ShapeDtypeStruct((1, width, columns), bf16),
            jax.ShapeDtypeStruct((1, units, width), bf16),
        ),
        in_specs=[vmem_spec] * 4,
        out_specs=(any_spec, any_spec),
        scratch_shapes=[pltpu.VMEM((width, columns), bf16), dma((width // 256 + 1,))],
        compiler_params=pltpu.CompilerParams(vmem_limit_bytes=LIMIT),
    )(*held)


def solution(mesh):
    placed = (
        P(("wide", "narrow"), None),
        P(("wide", "narrow")),
        P(("wide", "narrow")),
        P(("wide", "narrow"), None),
        P(("wide", "narrow"), None, None),
        P(("wide", "narrow"), None, None),
        P(("wide", "narrow"), None, None),
    )
    return jax.shard_map(
        body,
        mesh=mesh,
        in_specs=placed,
        out_specs=(P(("wide", "narrow"), None, None), P(("wide", "narrow"), None, None)),
        check_vma=False,
    )
```

```python
import functools

import jax
import jax.numpy as jnp
from jax import lax
from jax.experimental import pallas as pl
from jax.experimental.pallas import tpu as pltpu
from jax.sharding import PartitionSpec as P

second_correction = 1.0 - 0.95**10
bf16 = jnp.bfloat16
f32 = jnp.float32
LIMIT = 32 * 1024 * 1024


def mm(a, b, dims):
    return lax.dot_general(a, b, (dims, ((), ())), preferred_element_type=f32)


RELAYED = True
LENDS = 2
GATE = 1
PACK = (2, 3, 3)
FIRST_X = (2, 3, 3)
EARLY_D = (5, 3)
DIAGONAL_X = (4, 2, 2)
LATE_D = (2, 2, 2, 1, 1)


def spans(width, weights):
    unit = width // sum(weights)
    out, at = [], 0
    for weight in weights:
        out.append((at * unit, weight * unit))
        at += weight
    return out


def kernel(
    groups, wides, slot, relayed,
    ids_hbm, rw_hbm, tok_hbm, og_hbm, wgu_hbm, wdn_hbm, sm_hbm,
    acc_p, turned, pre_last, ustage,
    ids, rw, tok, og, wgu, wdn, sm, px, pd, rx, rd, lent, pre, hid, acc_d, moment, decay, turned_wdn,
    in_sem, send_sem, recv_sem, lent_sem, pass_sem, fsend_sem, frecv_sem, twice_sem, ready_sem,
):
    half = groups // 2
    width = tok.shape[1]
    hidden_units = wdn.shape[0]
    wide = lax.axis_index("wide")
    narrow = lax.axis_index("narrow")
    home = narrow // 2
    parity = lax.rem(narrow, 2)

    def along(step):
        return lax.rem(wide + wides + step, wides)

    def device(w, n):
        return {"wide": w, "narrow": n}

    def peer(j):
        return 2 * lax.rem(home + j, half) + parity

    odd = lax.rem(wide, 2) == 1
    even = jnp.logical_not(odd)
    sibling = device(wide, 2 * home + 1 - parity)

    order = [(0, 0), (1, 0)] + [(0, j) for j in range(2, half)]
    order += [(1, j) for j in range(1, half)] + [(0, 1)]
    early = list(range(half))
    late = list(range(half, groups))
    direct = 1
    diagonal = [b for b in late if order[b][0]]
    beside = [b for b in range(1, groups) if not order[b][0]]

    loads = []
    for i, (src, dst) in enumerate(
        (
            (tok_hbm, tok), (og_hbm, og), (wgu_hbm.at[0], wgu), (wdn_hbm.at[0], wdn),
            (sm_hbm.at[0], sm), (ids_hbm, ids), (rw_hbm, rw),
        )
    ):
        loads.append(pltpu.make_async_copy(src, dst, in_sem.at[i]))
    pieces = spans(width, PACK)
    for i, piece in enumerate(pieces):
        cols = pl.ds(*piece)
        loads.append(pltpu.make_async_copy(tok_hbm.at[:, cols], tok.at[:, cols], in_sem.at[7 + i]))
    for i in [5] + list(range(7, 7 + len(pieces))) + [6, 1]:
        loads[i].start()

    barrier = pltpu.get_barrier_semaphore()

    def signal(sem, partner):
        pl.semaphore_signal(sem, inc=1, device_id=partner, device_id_type=pl.DeviceIdType.MESH)

    signal(barrier, device(along(-1), narrow))
    for j in range(1, half):
        signal(barrier, device(wide, peer(j)))
    signal(barrier, sibling)
    if relayed:

        @pl.when(even)
        def _():
            signal(barrier, device(along(1), narrow))

    loads[5].wait()
    count = tok.shape[0]
    labels = ids[...]
    pad_groups = max(8, groups)
    onehot = (lax.broadcasted_iota(jnp.int32, (pad_groups, count), 0) == labels).astype(f32)
    before = (
        lax.broadcasted_iota(jnp.int32, (count, count), 0)
        < lax.broadcasted_iota(jnp.int32, (count, count), 1)
    ).astype(f32)
    counted = mm(onehot.astype(bf16), before.astype(bf16), ((1,), (0,)))
    within = jnp.sum(counted * onehot, axis=0, keepdims=True).astype(jnp.int32)
    slots = lax.broadcasted_iota(jnp.int32, (slot, count), 0)

    def select_of(b):
        kind, j = order[b]
        value = kind * half + lax.rem(home + j, half)
        return jnp.logical_and(labels == value, slots == within)

    near = late[-1]
    far = jnp.logical_and(wide == wides - 1, home > 0)
    swapped = jnp.logical_and(wide == 0, home > 0)
    near_swapped = jnp.logical_and(wide == 0, lax.rem(home + 1, half) > 0)
    lent_swapped = jnp.logical_and(along(2) == 0, home > 0)

    def rows(b, h, swap=None):
        if swap is None or b not in (direct, near):
            return pl.ds((2 * b + h) * slot, slot)
        at = jnp.where(swap, direct + near - b, b)
        return pl.ds(pl.multiple_of((2 * at + h) * slot, slot), slot)

    def remote(src, dst, s, r, dev):
        return pltpu.make_async_remote_copy(
            src_ref=src, dst_ref=dst, send_sem=s, recv_sem=r,
            device_id=dev, device_id_type=pl.DeviceIdType.MESH,
        )

    index, parts = {}, {}
    for b in range(1, groups):
        widths = (DIAGONAL_X if b in diagonal else FIRST_X, EARLY_D if b in early[2:] else LATE_D)
        for a in (0, 1):
            parts[b, a] = spans(width, widths[a])
            for c in range(len(parts[b, a])):
                index[b, a, c] = len(index)
    packed, received = (px, pd), (rx, rd)

    def cols_of(b, a, c):
        return pl.ds(*parts[b, a][c])

    def send(b, a, c):
        kind, j = order[b]
        cols = cols_of(b, a, c)
        return remote(
            packed[a].at[b - 1, :, cols],
            received[a].at[rows(b, 0, far if b == direct else near_swapped), cols],
            send_sem.at[2 if a == 0 and b == direct and c < lends else a], recv_sem.at[index[b, a, c]], device(along(kind), peer(j)),
        )

    lends = LENDS if relayed else 0

    def lend(c):
        cols = cols_of(direct, 0, c)
        return remote(
            px.at[direct - 1, :, cols], lent.at[:, cols],
            send_sem.at[2], lent_sem.at[c], device(along(-1), narrow),
        )

    def hand_on(c):
        cols = cols_of(direct, 0, c)
        return remote(
            lent.at[:, cols], rx.at[rows(direct, 0, lent_swapped), cols],
            pass_sem.at[0], recv_sem.at[index[direct, 0, c]], device(along(2), narrow),
        )

    def go_first(c):
        if relayed:

            @pl.when(odd)
            def _():
                lend(c).start()

            @pl.when(even)
            def _():
                send(direct, 0, c).start()
        else:
            send(direct, 0, c).start()

    def go_direct():
        for c in range(len(parts[direct, 1])):
            send(direct, 1, c).start()

    def go_rest():
        for c in range(lends, len(FIRST_X)):
            send(direct, 0, c).start()
        pl.when(jnp.logical_not(far))(go_direct)
        for a in (0, 1):
            for b in diagonal:
                for c in range(len(parts[b, a]) - a):
                    send(b, a, c).start()

    def first_sent():
        part = px.at[0, :, pl.ds(0, first_columns)]
        remote(part, part, send_sem.at[2], recv_sem.at[0], sibling).wait_send()

    held_back = jnp.logical_and(odd, wide != wides - 1)
    first_columns = sum(FIRST_X[:lends]) * width // sum(FIRST_X)

    final = len(LATE_D) - 1

    def send_twice(b):
        kind, j = order[b]
        cols, other = cols_of(b, 1, final), 2 * lax.rem(home + j, half) + 1 - parity
        return remote(
            pd.at[b - 1, :, cols], rd.at[rows(b, 1, near_swapped), cols],
            twice_sem.at[0], twice_sem.at[1 + b - half], device(along(kind), other),
        )

    def forward(b, a, c, late_one):
        cols = cols_of(b, a, c)
        x_sem = 0 if b < half else 2 + (b in beside)
        which = (4 + c if late_one else 1) if a else x_sem
        return remote(
            received[a].at[rows(b, 0, swapped), cols], received[a].at[rows(b, 1, swapped), cols],
            fsend_sem.at[a], frecv_sem.at[which], sibling,
        )

    def settle(which, a, blocks, cols=slice(None)):
        part = received[a].at[pl.ds(0, blocks * slot), cols]
        remote(part, part, fsend_sem.at[a], frecv_sem.at[which], sibling).wait_recv()

    selects = [select_of(b) for b in range(groups)]
    chosen = jnp.concatenate([s.astype(f32) for s in selects], axis=0).astype(bf16)

    def store(a, cols, block):
        for b in range(groups):
            piece = block[b * slot : (b + 1) * slot]
            if b:
                packed[a][b - 1, :, cols] = piece
            else:
                received[a][rows(0, 0), cols] = piece

    for n, (start, size) in enumerate(pieces):
        loads[7 + n].wait()
        cols = pl.ds(start, size)
        store(0, cols, mm(chosen, tok[:, cols], ((1,), (0,))).astype(bf16))
        if n == 0:
            near = 1 + half - 1 + 1
            if relayed:

                @pl.when(odd)
                def _():
                    pl.semaphore_wait(barrier, near + 1)

                @pl.when(even)
                def _():
                    pl.semaphore_wait(barrier, near)
            else:
                pl.semaphore_wait(barrier, near)
        for c, (at, extent) in enumerate(spans(width, FIRST_X)):
            if at + extent == start + size:
                if c < lends:
                    go_first(c)
                for b in beside:
                    send(b, 0, c).start()
        if n == 0:
            for j in range(1, half):
                signal(ready_sem, device(wide, peer(j)))
    for i in (2, 3, 4):
        loads[i].start()
    loads[6].wait()
    weights = rw[...]
    weight = jnp.concatenate(
        [jnp.sum(jnp.where(s, weights, 0.0), axis=1, keepdims=True) for s in selects], axis=0
    )
    loads[1].wait()
    for start, size in spans(width, PACK):
        cols = pl.ds(start, size)
        placed = mm(chosen, og[:, cols], ((1,), (0,)))
        store(1, cols, (weight * placed).astype(bf16))
    for b in beside:
        for c in range(len(parts[b, 1]) - (b in late)):
            send(b, 1, c).start()
    pl.when(near_swapped)(send(near, 1, final).start)
    if half > 1:
        pl.semaphore_wait(ready_sem, half - 1)
    if relayed:
        pl.when(jnp.logical_not(held_back))(go_rest)
    else:
        go_rest()
    for a in (0, 1):
        whole = received[a]
        remote(
            whole.at[rows(0, 0)], whole.at[rows(0, 1)],
            fsend_sem.at[a], frecv_sem.at[a], sibling,
        ).start()
    loads[2].wait()
    loads[3].wait()
    loads[4].wait()
    if relayed:

        @pl.when(even)
        def _():
            for c in range(lends):
                lend(c).wait_recv()
                hand_on(c).start()

    def project(r):
        projected = mm(rx[r, :], wgu[...], ((1,), (0,)))
        gate_pre = projected[:, :hidden_units]
        up_pre = projected[:, hidden_units:]
        logistic = jax.nn.sigmoid(gate_pre)
        swished = gate_pre * logistic
        hid[r, :] = (swished * up_pre).astype(bf16)
        return up_pre * logistic * (1.0 + gate_pre * (1.0 - logistic)), swished

    def finish(target, r, hidden_grad, factors):
        target[r, :] = jnp.concatenate(
            [hidden_grad * factors[0], hidden_grad * factors[1]], axis=1
        ).astype(bf16)

    def take(b, a, c, late_one):
        send(b, a, c).wait_recv()
        forward(b, a, c, late_one).start()

    def take_all(blocks, a):
        for b in blocks:
            for c in range(len(parts[b, a])):
                take(b, a, c, False)
                if relayed and b == direct and a == 0 and c < 2:
                    pl.when(jnp.logical_and(held_back, parity == c))(go_rest)

    take_all(early[1:], 0)
    take_all([late[-1]], 0)
    settle(0, 0, half)
    settle(3, 0, 1)

    def go_final(b):
        send(b, 1, final).start()
        send_twice(b).start()

    for b in diagonal:
        go_final(b)

    @pl.when(jnp.logical_not(near_swapped))
    def _():
        go_final(near)

    pl.when(far)(go_direct)
    first = pl.ds(0, half * 2 * slot)
    last = pl.ds(half * 2 * slot, half * 2 * slot)
    factors_first = project(first)
    take_all(early[2:], 1)
    rest = pl.ds(*parts[near, 1][final])

    @pl.when(jnp.logical_not(swapped))
    def _():
        take_all([direct], 1)

    @pl.when(swapped)
    def _():
        take_all([near], 1)

    moment[...] = (0.95 / second_correction) * sm[...].astype(f32)
    decay[...] = 0.1 * wdn[...].astype(f32)
    turned_wdn[...] = wdn[...].T
    settle(1, 1, half)
    finish(pre, first, mm(rd[first, :], wdn[...], ((1,), (1,))), factors_first)
    for i in range(width // 256):
        cols = pl.ds(i * 256, 256)
        acc_p[cols, :] = mm(rx[first, cols], pre[first, :], ((0,), (0,)))
        acc_d[:, cols] = mm(hid[first, :], rd[first, cols], ((0,), (0,)))
    take_all(diagonal, 0)

    def relay(c):
        for b in diagonal:
            take(b, 1, c, True)

        @pl.when(jnp.logical_not(swapped))
        def _():
            take(near, 1, c, True)

        @pl.when(swapped)
        def _():
            take(direct, 1, c, True)
            if c + 1 == final:
                take(direct, 1, final, True)

    @pl.when(parity == 1)
    def _():
        for c in range(final - 1):
            relay(c)

    settle(2, 0, half - 1)
    factors = project(last)
    turned[...] = rx[last, :].T
    turned_hid = hid[last, :].T

    @pl.when(parity == 1)
    def _():
        relay(final - 1)

    hidden_grad = jnp.zeros((half * 2 * slot, hidden_units), f32)
    late_d = spans(width, LATE_D)

    def add(c):
        cols = pl.ds(*late_d[c])
        return hidden_grad + mm(rd[last, cols], turned_wdn[cols, :], ((1,), (0,)))

    def update(c):
        cols = pl.ds(*late_d[c])
        total = acc_d[:, cols] + mm(turned_hid, rd[last, cols], ((1,), (0,)))
        second = moment[:, cols] + (0.05 / second_correction) * total * total
        root = second * lax.rsqrt(second)
        ustage[:, cols] = (total / (root + 1e-08) + decay[:, cols]).astype(bf16)

    for c in range(final):

        @pl.when(parity == 0)
        def _():
            relay(c)

        settle(4 + c, 1, half, pl.ds(*late_d[c]))
        hidden_grad = add(c)
        update(c)
    for b in diagonal:
        send(b, 1, final).wait_recv()
        send_twice(b).wait_recv()

    @pl.when(jnp.logical_not(swapped))
    def _():
        send(near, 1, final).wait_recv()
        send_twice(near).wait_recv()

    @pl.when(swapped)
    def _():
        settle(4 + final, 1, 1, rest)

    hidden_grad = add(final)
    finish(pre_last, slice(None), hidden_grad, factors)
    update(final)
    part = px.at[1:]
    remote(part, part, send_sem.at[0], recv_sem.at[0], sibling).wait_send()
    if relayed:
        first_sent()
        part = px.at[0, :, pl.ds(first_columns, width - first_columns)]
        remote(part, part, send_sem.at[0], recv_sem.at[0], sibling).wait_send()
    else:
        remote(px.at[0], px.at[0], send_sem.at[0], recv_sem.at[0], sibling).wait_send()
    remote(pd, pd, send_sem.at[1], recv_sem.at[0], sibling).wait_send()
    part = rx.at[pl.ds(0, groups * slot)]
    remote(part, part, fsend_sem.at[0], frecv_sem.at[0], sibling).wait_send()
    part, cols = rd.at[pl.ds(0, groups * slot)], pl.ds(0, late_d[final][0])
    remote(part.at[:, cols], part.at[:, cols], fsend_sem.at[1], frecv_sem.at[0], sibling).wait_send()
    part = rd.at[pl.ds(0, half * slot), rest]
    remote(part, part, fsend_sem.at[1], frecv_sem.at[0], sibling).wait_send()
    part = rd.at[pl.ds(0, slot), rest]

    @pl.when(jnp.logical_not(near_swapped))
    def _():
        remote(part, part, twice_sem.at[0], frecv_sem.at[0], sibling).wait_send()

    @pl.when(swapped)
    def _():
        remote(part, part, fsend_sem.at[1], frecv_sem.at[0], sibling).wait_send()

    for _ in diagonal:
        remote(part, part, twice_sem.at[0], frecv_sem.at[0], sibling).wait_send()
    if relayed:

        @pl.when(even)
        def _():
            part = lent.at[:, pl.ds(0, first_columns)]
            remote(part, part, pass_sem.at[0], recv_sem.at[0], sibling).wait_send()


def final_kernel(acc_p, turned, pre_last, update, gout, uout, gstage, out_sem):
    tiles = acc_p.shape[0] // 256
    outs = [pltpu.make_async_copy(update, uout.at[0], out_sem.at[tiles])]
    outs[0].start()
    for i in range(tiles):
        r = pl.ds(i * 256, 256)
        gstage[r, :] = (acc_p[r, :] + mm(turned[r, :], pre_last[...], ((1,), (0,)))).astype(bf16)
        copy = pltpu.make_async_copy(gstage.at[r], gout.at[0, r], out_sem.at[i])
        copy.start()
        outs.append(copy)
    for copy in outs:
        copy.wait()


def body(tokens, expert_ids, route_weights, out_grad, w_gate_up, w_down, second_moment):
    groups = lax.axis_size("narrow")
    wides = lax.axis_size("wide")
    count, width = tokens.shape
    cap = 3 * count // (2 * groups)
    slot = -(-cap // 16) * 16
    columns = w_gate_up.shape[2]
    units = w_down.shape[1]
    half = groups // 2
    all_rows = groups * 2 * slot
    last_rows = half * 2 * slot
    relayed = RELAYED and wides % 2 == 0 and wides >= 4
    chunks = (groups - 1) * (len(FIRST_X) + len(LATE_D))
    dma = pltpu.SemaphoreType.DMA
    any_spec = pl.BlockSpec(memory_space=pl.ANY)
    vmem_spec = pl.BlockSpec(memory_space=pltpu.VMEM)
    held = pl.pallas_call(
        functools.partial(kernel, groups, wides, slot, relayed),
        out_shape=(
            pltpu.VMEM((width, columns), f32),
            pltpu.VMEM((width, last_rows), bf16),
            pltpu.VMEM((last_rows, columns), bf16),
            pltpu.VMEM((units, width), bf16),
        ),
        in_specs=[any_spec] * 7,
        out_specs=(vmem_spec,) * 4,
        scratch_shapes=[
            pltpu.VMEM((1, count), jnp.int32),
            pltpu.VMEM((1, count), f32),
            pltpu.VMEM((count, width), bf16),
            pltpu.VMEM((count, width), bf16),
            pltpu.VMEM((width, columns), bf16),
            pltpu.VMEM((units, width), bf16),
            pltpu.VMEM((units, width), bf16),
            pltpu.VMEM((groups - 1, slot, width), bf16),
            pltpu.VMEM((groups - 1, slot, width), bf16),
            pltpu.VMEM((all_rows, width), bf16),
            pltpu.VMEM((all_rows, width), bf16),
            pltpu.VMEM((slot, width), bf16),
            pltpu.VMEM((last_rows, columns), bf16),
            pltpu.VMEM((all_rows, units), bf16),
            pltpu.VMEM((units, width), f32),
            pltpu.VMEM((units, width), f32),
            pltpu.VMEM((units, width), f32),
            pltpu.VMEM((width, units), bf16),
            dma((7 + len(PACK),)), dma((3,)), dma((chunks,)), dma((len(FIRST_X),)), dma((1,)), dma((2,)),
            dma((4 + len(LATE_D),)), dma((1 + half,)), pltpu.SemaphoreType.REGULAR,
        ],
        compiler_params=pltpu.CompilerParams(
            collective_id=0, has_side_effects=True, vmem_limit_bytes=LIMIT
        ),
    )(
        *(
            pltpu.with_memory_space_constraint(value, pltpu.HBM)
            for value in (
                expert_ids.reshape(1, count), route_weights.reshape(1, count),
                tokens, out_grad, w_gate_up, w_down, second_moment,
            )
        ),
    )
    return pl.pallas_call(
        final_kernel,
        out_shape=(
            jax.ShapeDtypeStruct((1, width, columns), bf16),
            jax.ShapeDtypeStruct((1, units, width), bf16),
        ),
        in_specs=[vmem_spec] * 4,
        out_specs=(any_spec, any_spec),
        scratch_shapes=[pltpu.VMEM((width, columns), bf16), dma((width // 256 + 1,))],
        compiler_params=pltpu.CompilerParams(vmem_limit_bytes=LIMIT),
    )(*held)


def solution(mesh):
    placed = (
        P(("wide", "narrow"), None),
        P(("wide", "narrow")),
        P(("wide", "narrow")),
        P(("wide", "narrow"), None),
        P(("wide", "narrow"), None, None),
        P(("wide", "narrow"), None, None),
        P(("wide", "narrow"), None, None),
    )
    return jax.shard_map(
        body,
        mesh=mesh,
        in_specs=placed,
        out_specs=(P(("wide", "narrow"), None, None), P(("wide", "narrow"), None, None)),
        check_vma=False,
    )
```

```python
import functools

import jax
import jax.numpy as jnp
from jax import lax
from jax.experimental import pallas as pl
from jax.experimental.pallas import tpu as pltpu
from jax.sharding import PartitionSpec as P

second_correction = 1.0 - 0.95**10
bf16 = jnp.bfloat16
f32 = jnp.float32
LIMIT = 32 * 1024 * 1024


def mm(a, b, dims):
    return lax.dot_general(a, b, (dims, ((), ())), preferred_element_type=f32)


LENDS = 2
PACK = (2, 3, 3)
FIRST_X = (2, 3, 3)
EARLY_D = (5, 3)
DIAGONAL_X = (4, 2, 2)
LATE_D = (2, 2, 2, 1, 1)


def spans(width, weights):
    unit = width // sum(weights)
    out, at = [], 0
    for weight in weights:
        out.append((at * unit, weight * unit))
        at += weight
    return out


def kernel(
    groups, wides, slot, relayed,
    ids_hbm, rw_hbm, tok_hbm, og_hbm, wgu_hbm, wdn_hbm, sm_hbm,
    acc_p, turned, pre_last, ustage,
    ids, rw, tok, og, wgu, wdn, sm, px, pd, rx, rd, lent, pre, hid, acc_d, moment, decay, turned_wdn,
    in_sem, sent_sem, recv_sem, lent_sem, frecv_sem, twice_sem, ready_sem,
):
    half = groups // 2
    width = tok.shape[1]
    hidden_units = wdn.shape[0]
    wide = lax.axis_index("wide")
    narrow = lax.axis_index("narrow")
    home = narrow // 2
    parity = lax.rem(narrow, 2)

    def along(step):
        return lax.rem(wide + wides + step, wides)

    def device(w, n):
        return {"wide": w, "narrow": n}

    def peer(j, other=0):
        return 2 * lax.rem(home + j, half) + lax.rem(parity + other, 2)

    def crossed(step, j):
        same = jnp.logical_and(along(step) == 0, lax.rem(home + j, half) == 0)
        return jnp.where(same, 0, 1)

    def target(step, j, other=0):
        return device(along(step), peer(j, crossed(step, j) + other))

    def source(step, j):
        return device(along(step), peer(j, crossed(0, 0)))

    odd = lax.rem(wide, 2) == 1
    even = jnp.logical_not(odd)
    sibling = device(wide, 2 * home + 1 - parity)
    leads = parity != crossed(0, 0)

    order = [(0, 0), (1, 0)] + [(0, j) for j in range(2, half)]
    order += [(1, j) for j in range(1, half)] + [(0, 1)]
    early = list(range(half))
    late = list(range(half, groups))
    direct = 1
    diagonal = [b for b in late if order[b][0]]
    beside = [b for b in range(1, groups) if not order[b][0]]

    pieces = spans(width, PACK)
    loads = {}

    def load(name, src, dst, i):
        loads[name] = pltpu.make_async_copy(src, dst, in_sem.at[i])

    load("ids", ids_hbm, ids, 0)
    for n, piece in enumerate(pieces):
        load(n, tok_hbm.at[:, pl.ds(*piece)], tok.at[:, pl.ds(*piece)], 6 + n)
    load("rw", rw_hbm, rw, 1)
    load("og", og_hbm, og, 2)
    for copy in loads.values():
        copy.start()
    load("wgu", wgu_hbm.at[0], wgu, 3)
    load("wdn", wdn_hbm.at[0], wdn, 4)
    load("sm", sm_hbm.at[0], sm, 5)

    barrier = pltpu.get_barrier_semaphore()

    def signal(sem, partner):
        pl.semaphore_signal(sem, inc=1, device_id=partner, device_id_type=pl.DeviceIdType.MESH)

    signal(barrier, source(-1, 0))
    for j in range(1, half):
        signal(barrier, source(0, j))
        signal(barrier, device(wide, peer(j, crossed(0, 0) + 1)))
    signal(barrier, sibling)
    if relayed:

        @pl.when(even)
        def _():
            signal(barrier, device(along(1), narrow))

    loads["ids"].wait()
    count = tok.shape[0]
    labels = ids[...]
    pad_groups = max(8, groups)
    onehot = (lax.broadcasted_iota(jnp.int32, (pad_groups, count), 0) == labels).astype(f32)
    before = (
        lax.broadcasted_iota(jnp.int32, (count, count), 0)
        < lax.broadcasted_iota(jnp.int32, (count, count), 1)
    ).astype(f32)
    counted = mm(onehot.astype(bf16), before.astype(bf16), ((1,), (0,)))
    within = jnp.sum(counted * onehot, axis=0, keepdims=True).astype(jnp.int32)
    slots = lax.broadcasted_iota(jnp.int32, (slot, count), 0)

    def select_of(b):
        kind, j = order[b]
        value = kind * half + lax.rem(home + j, half)
        return jnp.logical_and(labels == value, slots == within)

    near = late[-1]
    far = jnp.logical_and(wide == wides - 1, home > 0)
    swapped = jnp.logical_and(wide == 0, home > 0)
    near_swapped = jnp.logical_and(wide == 0, lax.rem(home + 1, half) > 0)
    plain = jnp.logical_and(wide == 0, home == 0)
    lent_swapped = jnp.logical_and(along(2) == 0, home > 0)

    def rows(b, h, swap=None):
        if swap is None or b not in (direct, near):
            return pl.ds((2 * b + h) * slot, slot)
        at = jnp.where(swap, direct + near - b, b)
        return pl.ds(pl.multiple_of((2 * at + h) * slot, slot), slot)

    def remote(src, dst, s, r, dev):
        return pltpu.make_async_remote_copy(
            src_ref=src, dst_ref=dst, send_sem=s, recv_sem=r,
            device_id=dev, device_id_type=pl.DeviceIdType.MESH,
        )

    index, parts, used = {}, {}, 0
    for b in range(1, groups):
        widths = (DIAGONAL_X if b in diagonal else FIRST_X, EARLY_D if b in early[2:] else LATE_D)
        for a in (0, 1):
            parts[b, a] = spans(width, widths[a])
            one = b in beside if a == 0 else b in early
            for c in range(len(parts[b, a])):
                index[b, a, c] = used if one else used + c
            used += 1 if one else len(parts[b, a])

    packed, received = (px, pd), (rx, rd)

    def cols_of(b, a, c):
        return pl.ds(*parts[b, a][c])

    def slot_of(b, a, c, swap):
        if a and b in (direct, near):
            return jnp.where(swap, index[direct + near - b, 1, c], index[b, 1, c])
        return index[b, a, c]

    def send(b, a, c):
        kind, j = order[b]
        cols, swap = cols_of(b, a, c), far if b == direct else near_swapped
        return remote(
            packed[a].at[b - 1, :, cols], received[a].at[rows(b, 0, swap), cols],
            sent_sem.at[0], recv_sem.at[slot_of(b, a, c, swap)], target(kind, j),
        )

    lends = LENDS if relayed else 0

    def lend(c):
        cols = cols_of(direct, 0, c)
        return remote(
            px.at[direct - 1, :, cols], lent.at[:, cols],
            sent_sem.at[0], lent_sem.at[c], device(along(-1), narrow),
        )

    def hand_on(c):
        cols = cols_of(direct, 0, c)
        return remote(
            lent.at[:, cols], rx.at[rows(direct, 0, lent_swapped), cols],
            sent_sem.at[0], recv_sem.at[index[direct, 0, c]], target(2, 0),
        )

    def go_first(c):
        if relayed:

            @pl.when(odd)
            def _():
                lend(c).start()

            @pl.when(even)
            def _():
                send(direct, 0, c).start()
        else:
            send(direct, 0, c).start()

    def go_direct():
        for c in range(len(parts[direct, 1])):
            send(direct, 1, c).start()

    def go_rest():
        for c in range(lends, len(FIRST_X)):
            send(direct, 0, c).start()
        pl.when(jnp.logical_not(far))(go_direct)
        for a in (0, 1):
            for b in diagonal:
                for c in range(len(parts[b, a]) - a):
                    send(b, a, c).start()

    held_back = jnp.logical_and(odd, wide != wides - 1)
    first_columns = sum(FIRST_X[:lends]) * width // sum(FIRST_X)

    final = len(LATE_D) - 1

    def send_twice(b):
        kind, j = order[b]
        cols = cols_of(b, 1, final)
        return remote(
            pd.at[b - 1, :, cols], rd.at[rows(b, 1, near_swapped), cols],
            sent_sem.at[0], twice_sem.at[0], target(kind, j, 1),
        )

    def forward(b, a, cols, which):
        return remote(
            received[a].at[rows(b, 0, swapped), cols], received[a].at[rows(b, 1, swapped), cols],
            sent_sem.at[0], frecv_sem.at[which], sibling,
        )

    def arrived(part, sem):
        return remote(part, part, sent_sem.at[0], sem, sibling)

    def settle(which, a, blocks, cols=slice(None)):
        arrived(received[a].at[pl.ds(0, blocks * slot), cols], frecv_sem.at[which]).wait_recv()

    selects = [select_of(b) for b in range(groups)]
    chosen = jnp.concatenate([s.astype(f32) for s in selects], axis=0).astype(bf16)

    def store(a, cols, block):
        for b in range(groups):
            piece = block[b * slot : (b + 1) * slot]
            if b:
                packed[a][b - 1, :, cols] = piece
            else:
                received[a][rows(0, 0), cols] = piece

    for n, (start, size) in enumerate(pieces):
        loads[n].wait()
        cols = pl.ds(start, size)
        store(0, cols, mm(chosen, tok[:, cols], ((1,), (0,))).astype(bf16))
        if n == 0:
            entered = 1 + 2 * (half - 1) + 1
            if relayed:

                @pl.when(odd)
                def _():
                    pl.semaphore_wait(barrier, entered + 1)

                @pl.when(even)
                def _():
                    pl.semaphore_wait(barrier, entered)
            else:
                pl.semaphore_wait(barrier, entered)
        for c, (at, extent) in enumerate(spans(width, FIRST_X)):
            if at + extent == start + size:
                if c < lends:
                    go_first(c)
                for b in beside:
                    send(b, 0, c).start()
        if n == 0:
            for j in range(1, half):
                signal(ready_sem, device(wide, peer(j)))
    for name in ("wgu", "wdn", "sm"):
        loads[name].start()
    loads["rw"].wait()
    loads["og"].wait()
    weights = rw[...]
    weight = jnp.concatenate(
        [jnp.sum(jnp.where(s, weights, 0.0), axis=1, keepdims=True) for s in selects], axis=0
    )
    for start, size in spans(width, PACK):
        cols = pl.ds(start, size)
        placed = mm(chosen, og[:, cols], ((1,), (0,)))
        store(1, cols, (weight * placed).astype(bf16))
    for b in beside:
        for c in range(len(parts[b, 1]) - (b in late)):
            send(b, 1, c).start()
    pl.when(near_swapped)(send(near, 1, final).start)
    if half > 1:
        pl.semaphore_wait(ready_sem, half - 1)
    if relayed:
        pl.when(jnp.logical_not(held_back))(go_rest)
    else:
        go_rest()
    for a in (0, 1):
        forward(0, a, slice(None), a).start()
    if relayed:

        @pl.when(even)
        def _():
            for c in range(lends):
                lend(c).wait_recv()
                hand_on(c).start()

    def project(r):
        projected = mm(rx[r, :], wgu[...], ((1,), (0,)))
        gate_pre = projected[:, :hidden_units]
        up_pre = projected[:, hidden_units:]
        logistic = jax.nn.sigmoid(gate_pre)
        swished = gate_pre * logistic
        hid[r, :] = (swished * up_pre).astype(bf16)
        return up_pre * logistic * (1.0 + gate_pre * (1.0 - logistic)), swished

    def finish(target, r, hidden_grad, factors):
        target[r, :] = jnp.concatenate(
            [hidden_grad * factors[0], hidden_grad * factors[1]], axis=1
        ).astype(bf16)

    def take(b, a, c, which):
        cols = cols_of(b, a, c)
        i = index[near if b == direct and a and which > 2 else b, a, c]
        arrived(received[a].at[rows(b, 0, swapped), cols], recv_sem.at[i]).wait_recv()
        forward(b, a, cols, which).start()

    def take_whole(b, a, which):
        i = index[direct if b == near and a else b, a, 0]
        arrived(received[a].at[rows(b, 0, swapped)], recv_sem.at[i]).wait_recv()
        forward(b, a, slice(None), which).start()

    for c in range(len(FIRST_X)):
        take(direct, 0, c, 0)
        if relayed and c < 2:
            ready = leads if c else jnp.logical_not(leads)
            pl.when(jnp.logical_and(held_back, ready))(go_rest)
    for b in beside:
        take_whole(b, 0, 0)
    settle(0, 0, half + 1)

    def single(b):
        return jnp.logical_and(wide == wides - 1, lax.rem(home + order[b][1], half) == 0)

    def go_final(b):
        send(b, 1, final).start()
        send_twice(b).start()

    for b in diagonal:
        send(b, 1, final).start()
        pl.when(jnp.logical_not(single(b)))(send_twice(b).start)

    @pl.when(jnp.logical_not(near_swapped))
    def _():
        go_final(near)

    pl.when(far)(go_direct)
    first = pl.ds(0, half * 2 * slot)
    last = pl.ds(half * 2 * slot, half * 2 * slot)
    for name in ("wgu", "wdn", "sm"):
        loads[name].wait()
    factors_first = project(first)
    rest = pl.ds(*parts[near, 1][final])
    for b in early[2:]:
        take_whole(b, 1, 1)

    @pl.when(jnp.logical_not(swapped))
    def _():
        take_whole(direct, 1, 1)

    @pl.when(swapped)
    def _():
        take_whole(near, 1, 1)

    moment[...] = (0.95 / second_correction) * sm[...].astype(f32)
    decay[...] = 0.1 * wdn[...].astype(f32)
    turned_wdn[...] = wdn[...].T
    settle(1, 1, half)
    finish(pre, first, mm(rd[first, :], wdn[...], ((1,), (1,))), factors_first)
    for i in range(width // 256):
        cols = pl.ds(i * 256, 256)
        acc_p[cols, :] = mm(rx[first, cols], pre[first, :], ((0,), (0,)))
        acc_d[:, cols] = mm(hid[first, :], rd[first, cols], ((0,), (0,)))
    for b in diagonal:
        for c in range(len(DIAGONAL_X)):
            take(b, 0, c, 2)

    def relay(c):
        for b in diagonal:
            take(b, 1, c, 3 + c)
            if c + 1 == final:
                pl.when(plain)(lambda b=b: take(b, 1, final, 3 + final))

        @pl.when(jnp.logical_not(swapped))
        def _():
            take(near, 1, c, 3 + c)

        @pl.when(swapped)
        def _():
            take(direct, 1, c, 3 + c)
            if c + 1 == final:
                take(direct, 1, final, 3 + final)

    @pl.when(leads)
    def _():
        for c in range(final - 1):
            relay(c)

    settle(2, 0, half - 1)
    factors = project(last)
    turned[...] = rx[last, :].T
    turned_hid = hid[last, :].T

    @pl.when(leads)
    def _():
        relay(final - 1)

    hidden_grad = jnp.zeros((half * 2 * slot, hidden_units), f32)
    late_d = spans(width, LATE_D)

    def add(c):
        cols = pl.ds(*late_d[c])
        return hidden_grad + mm(rd[last, cols], turned_wdn[cols, :], ((1,), (0,)))

    def update(c):
        cols = pl.ds(*late_d[c])
        total = acc_d[:, cols] + mm(turned_hid, rd[last, cols], ((1,), (0,)))
        second = moment[:, cols] + (0.05 / second_correction) * total * total
        root = second * lax.rsqrt(second)
        ustage[:, cols] = (total / (root + 1e-08) + decay[:, cols]).astype(bf16)

    for c in range(final):

        @pl.when(jnp.logical_not(leads))
        def _():
            relay(c)

        settle(3 + c, 1, half, pl.ds(*late_d[c]))
        hidden_grad = add(c)
        update(c)
    tail = rd.at[pl.ds(0, slot), rest]

    @pl.when(jnp.logical_not(plain))
    def _():
        for b in diagonal:
            arrived(tail, recv_sem.at[index[b, 1, final]]).wait_recv()

    pl.when(plain)(lambda: settle(3 + final, 1, half - 1, rest))

    @pl.when(jnp.logical_not(swapped))
    def _():
        arrived(tail, recv_sem.at[index[near, 1, final]]).wait_recv()

    @pl.when(swapped)
    def _():
        settle(3 + final, 1, 1, rest)

    def doubled(blocks, condition):
        @pl.when(condition)
        def _():
            arrived(rd.at[pl.ds(0, blocks * slot), rest], twice_sem.at[0]).wait_recv()

    ordinary = jnp.logical_not(jnp.logical_or(plain, swapped))
    doubled(half, ordinary)
    doubled(1, plain)
    if half > 1:
        doubled(half - 1, swapped)
    hidden_grad = add(final)
    finish(pre_last, slice(None), hidden_grad, factors)
    update(final)
    def sent(part):
        arrived(part, recv_sem.at[0]).wait_send()

    most = pl.ds(0, late_d[final][0])
    sent(px)
    sent(pd)
    sent(rx.at[pl.ds(0, groups * slot)])
    sent(rd.at[pl.ds(0, groups * slot), most])
    sent(rd.at[pl.ds(0, half * slot), rest])
    for b in diagonal:
        pl.when(jnp.logical_not(single(b)))(lambda: sent(tail))
        pl.when(plain)(lambda: sent(tail))
    unless_near = jnp.logical_not(near_swapped)
    pl.when(unless_near)(lambda: sent(tail))
    pl.when(swapped)(lambda: sent(tail))
    if relayed:
        pl.when(even)(lambda: sent(lent.at[:, pl.ds(0, first_columns)]))


def final_kernel(acc_p, turned, pre_last, update, gout, uout, gstage, out_sem):
    tiles = acc_p.shape[0] // 256
    outs = [pltpu.make_async_copy(update, uout.at[0], out_sem.at[0])]
    outs[0].start()
    for i in range(tiles):
        r = pl.ds(i * 256, 256)
        gstage[r, :] = (acc_p[r, :] + mm(turned[r, :], pre_last[...], ((1,), (0,)))).astype(bf16)
        copy = pltpu.make_async_copy(gstage.at[r], gout.at[0, r], out_sem.at[0])
        copy.start()
        outs.append(copy)
    for copy in outs:
        copy.wait()


def body(tokens, expert_ids, route_weights, out_grad, w_gate_up, w_down, second_moment):
    groups = lax.axis_size("narrow")
    wides = lax.axis_size("wide")
    count, width = tokens.shape
    cap = 3 * count // (2 * groups)
    slot = -(-cap // 16) * 16
    columns = w_gate_up.shape[2]
    units = w_down.shape[1]
    half = groups // 2
    all_rows = groups * 2 * slot
    last_rows = half * 2 * slot
    relayed = wides % 2 == 0 and wides >= 4
    chunks = len(FIRST_X) + half + half - 1 + (half - 1) * len(DIAGONAL_X) + half * len(LATE_D)
    dma = pltpu.SemaphoreType.DMA
    any_spec = pl.BlockSpec(memory_space=pl.ANY)
    vmem_spec = pl.BlockSpec(memory_space=pltpu.VMEM)
    held = pl.pallas_call(
        functools.partial(kernel, groups, wides, slot, relayed),
        out_shape=(
            pltpu.VMEM((width, columns), f32),
            pltpu.VMEM((width, last_rows), bf16),
            pltpu.VMEM((last_rows, columns), bf16),
            pltpu.VMEM((units, width), bf16),
        ),
        in_specs=[any_spec] * 7,
        out_specs=(vmem_spec,) * 4,
        scratch_shapes=[
            pltpu.VMEM((1, count), jnp.int32),
            pltpu.VMEM((1, count), f32),
            pltpu.VMEM((count, width), bf16),
            pltpu.VMEM((count, width), bf16),
            pltpu.VMEM((width, columns), bf16),
            pltpu.VMEM((units, width), bf16),
            pltpu.VMEM((units, width), bf16),
            pltpu.VMEM((groups - 1, slot, width), bf16),
            pltpu.VMEM((groups - 1, slot, width), bf16),
            pltpu.VMEM((all_rows, width), bf16),
            pltpu.VMEM((all_rows, width), bf16),
            pltpu.VMEM((slot, width), bf16),
            pltpu.VMEM((last_rows, columns), bf16),
            pltpu.VMEM((all_rows, units), bf16),
            pltpu.VMEM((units, width), f32),
            pltpu.VMEM((units, width), f32),
            pltpu.VMEM((units, width), f32),
            pltpu.VMEM((width, units), bf16),
            dma((6 + len(PACK),)), dma((1,)), dma((chunks,)), dma((max(LENDS, 1),)),
            dma((3 + len(LATE_D),)), dma((1,)), pltpu.SemaphoreType.REGULAR,
        ],
        compiler_params=pltpu.CompilerParams(
            collective_id=0, has_side_effects=True, vmem_limit_bytes=LIMIT
        ),
    )(
        *(
            pltpu.with_memory_space_constraint(value, pltpu.HBM)
            for value in (
                expert_ids.reshape(1, count), route_weights.reshape(1, count),
                tokens, out_grad, w_gate_up, w_down, second_moment,
            )
        ),
    )
    return pl.pallas_call(
        final_kernel,
        out_shape=(
            jax.ShapeDtypeStruct((1, width, columns), bf16),
            jax.ShapeDtypeStruct((1, units, width), bf16),
        ),
        in_specs=[vmem_spec] * 4,
        out_specs=(any_spec, any_spec),
        scratch_shapes=[pltpu.VMEM((width, columns), bf16), dma((1,))],
        compiler_params=pltpu.CompilerParams(vmem_limit_bytes=LIMIT),
    )(*held)


def solution(mesh):
    placed = (
        P(("wide", "narrow"), None),
        P(("wide", "narrow")),
        P(("wide", "narrow")),
        P(("wide", "narrow"), None),
        P(("wide", "narrow"), None, None),
        P(("wide", "narrow"), None, None),
        P(("wide", "narrow"), None, None),
    )
    return jax.shard_map(
        body,
        mesh=mesh,
        in_specs=placed,
        out_specs=(P(("wide", "narrow"), None, None), P(("wide", "narrow"), None, None)),
        check_vma=False,
    )
```

```python
import functools

import jax
import jax.numpy as jnp
from jax import lax
from jax.experimental import pallas as pl
from jax.experimental.pallas import tpu as pltpu
from jax.sharding import PartitionSpec as P

second_correction = 1.0 - 0.95**10
bf16 = jnp.bfloat16
f32 = jnp.float32
LIMIT = 32 * 1024 * 1024


def mm(a, b, dims):
    return lax.dot_general(a, b, (dims, ((), ())), preferred_element_type=f32)


LENDS = 2
AHEAD = 1
TURN = 1
PACK = (2, 3, 3)
FIRST_X = (2, 3, 3)
EARLY_D = (5, 3)
DIAGONAL_X = (4, 2, 2)
LATE_D = (3, 2, 2, 1)


def spans(width, weights):
    unit = width // sum(weights)
    out, at = [], 0
    for weight in weights:
        out.append((at * unit, weight * unit))
        at += weight
    return out


def kernel(
    groups, wides, slot, relayed,
    ids_hbm, rw_hbm, tok_hbm, og_hbm, wgu_hbm, wdn_hbm, sm_hbm,
    acc_p, turned, pre_last, ustage,
    ids, rw, tok, og, wgu, wdn, sm, px, pd, rx, rd, lent, pre, hid, acc_d, moment, decay, turned_wdn,
    in_sem, sent_sem, recv_sem, lent_sem, frecv_sem, ready_sem,
):
    half = groups // 2
    width = tok.shape[1]
    hidden_units = wdn.shape[0]
    wide = lax.axis_index("wide")
    narrow = lax.axis_index("narrow")
    home = narrow // 2
    parity = lax.rem(narrow, 2)

    def along(step):
        return lax.rem(wide + wides + step, wides)

    def device(w, n):
        return {"wide": w, "narrow": n}

    def peer(j, other=0):
        return 2 * lax.rem(home + j, half) + lax.rem(parity + other, 2)

    def crossed(step, j):
        same = jnp.logical_and(along(step) == 0, lax.rem(home + j, half) == 0)
        return jnp.where(same, 0, 1)

    def target(step, j, other=0):
        return device(along(step), peer(j, crossed(step, j) + other))

    def source(step, j):
        return device(along(step), peer(j, crossed(0, 0)))

    odd = lax.rem(wide, 2) == 1
    even = jnp.logical_not(odd)
    sibling = device(wide, 2 * home + 1 - parity)
    leads = parity != crossed(0, 0)

    order = [(0, 0), (1, 0)] + [(0, j) for j in range(2, half)]
    order += [(0, 1)] + [(1, j) for j in range(1, half)]
    early = list(range(half))
    late = list(range(half, groups))
    direct = 1
    diagonal = [b for b in late if order[b][0]]
    beside = [b for b in range(1, groups) if not order[b][0]]

    pieces = spans(width, PACK)
    loads = {}

    def load(name, src, dst, i):
        loads[name] = pltpu.make_async_copy(src, dst, in_sem.at[i])

    load("ids", ids_hbm, ids, 0)
    for n, piece in enumerate(pieces):
        load(n, tok_hbm.at[:, pl.ds(*piece)], tok.at[:, pl.ds(*piece)], 6 + n)
    load("rw", rw_hbm, rw, 1)
    load("og", og_hbm, og, 2)
    for copy in loads.values():
        copy.start()
    load("wgu", wgu_hbm.at[0], wgu, 3)
    load("wdn", wdn_hbm.at[0], wdn, 4)
    load("sm", sm_hbm.at[0], sm, 5)

    barrier = pltpu.get_barrier_semaphore()

    def signal(sem, partner):
        pl.semaphore_signal(sem, inc=1, device_id=partner, device_id_type=pl.DeviceIdType.MESH)

    signal(barrier, source(-1, 0))
    for j in range(1, half):
        signal(barrier, source(0, j))
        signal(barrier, device(wide, peer(j, crossed(0, 0) + 1)))
    signal(barrier, sibling)
    if relayed:

        @pl.when(even)
        def _():
            signal(barrier, device(along(1), narrow))

    loads["ids"].wait()
    count = tok.shape[0]
    labels = ids[...]
    pad_groups = max(8, groups)
    onehot = (lax.broadcasted_iota(jnp.int32, (pad_groups, count), 0) == labels).astype(f32)
    before = (
        lax.broadcasted_iota(jnp.int32, (count, count), 0)
        < lax.broadcasted_iota(jnp.int32, (count, count), 1)
    ).astype(f32)
    counted = mm(onehot.astype(bf16), before.astype(bf16), ((1,), (0,)))
    within = jnp.sum(counted * onehot, axis=0, keepdims=True).astype(jnp.int32)
    slots = lax.broadcasted_iota(jnp.int32, (slot, count), 0)

    def select_of(b):
        kind, j = order[b]
        value = kind * half + lax.rem(home + j, half)
        return jnp.logical_and(labels == value, slots == within)

    near = half
    far = jnp.logical_and(wide == wides - 1, home > 0)
    swapped = jnp.logical_and(wide == 0, home > 0)
    near_swapped = jnp.logical_and(wide == 0, lax.rem(home + 1, half) > 0)
    lent_swapped = jnp.logical_and(along(2) == 0, home > 0)

    def rows(b, h, swap=None):
        if swap is None or b not in (direct, near):
            return pl.ds((2 * b + h) * slot, slot)
        at = jnp.where(swap, direct + near - b, b)
        return pl.ds(pl.multiple_of((2 * at + h) * slot, slot), slot)

    def remote(src, dst, s, r, dev):
        return pltpu.make_async_remote_copy(
            src_ref=src, dst_ref=dst, send_sem=s, recv_sem=r,
            device_id=dev, device_id_type=pl.DeviceIdType.MESH,
        )

    index, parts, used = {}, {}, 0
    for b in range(1, groups):
        widths = (DIAGONAL_X if b in diagonal else FIRST_X, EARLY_D if b in early[2:] else LATE_D)
        for a in (0, 1):
            parts[b, a] = spans(width, widths[a])
            one = b in beside if a == 0 else b in early
            for c in range(len(parts[b, a])):
                index[b, a, c] = used if one else used + c
            used += 1 if one else len(parts[b, a])

    packed, received = (px, pd), (rx, rd)

    def cols_of(b, a, c):
        return pl.ds(*parts[b, a][c])

    def slot_of(b, a, c, swap):
        if a and b in (direct, near):
            return jnp.where(swap, index[direct + near - b, 1, c], index[b, 1, c])
        return index[b, a, c]

    def send(b, a, c):
        kind, j = order[b]
        cols, swap = cols_of(b, a, c), far if b == direct else near_swapped
        return remote(
            packed[a].at[b - 1, :, cols], received[a].at[rows(b, 0, swap), cols],
            sent_sem.at[0], recv_sem.at[slot_of(b, a, c, swap)], target(kind, j),
        )

    lends = LENDS if relayed else 0

    def lend(c):
        cols = cols_of(direct, 0, c)
        return remote(
            px.at[direct - 1, :, cols], lent.at[:, cols],
            sent_sem.at[0], lent_sem.at[c], device(along(-1), narrow),
        )

    def hand_on(c):
        cols = cols_of(direct, 0, c)
        return remote(
            lent.at[:, cols], rx.at[rows(direct, 0, lent_swapped), cols],
            sent_sem.at[0], recv_sem.at[index[direct, 0, c]], target(2, 0),
        )

    def go_first(c):
        if relayed:

            @pl.when(odd)
            def _():
                lend(c).start()

            @pl.when(even)
            def _():
                send(direct, 0, c).start()
        else:
            send(direct, 0, c).start()

    def go_direct():
        for c in range(len(parts[direct, 1])):
            send(direct, 1, c).start()

    def go_more():
        for c in range(lends, len(FIRST_X)):
            send(direct, 0, c).start()

    held_back = jnp.logical_and(odd, wide != wides - 1) if relayed else wide < 0

    def go_rest():
        pl.when(held_back)(go_more)
        pl.when(jnp.logical_not(far))(go_direct)
        for a in (0, 1):
            for b in diagonal:
                for c in range(len(parts[b, a])):
                    send(b, a, c).start()

    first_columns = sum(FIRST_X[:lends]) * width // sum(FIRST_X)

    final = len(LATE_D)

    def forward(b, a, cols, which):
        return remote(
            received[a].at[rows(b, 0, swapped), cols], received[a].at[rows(b, 1, swapped), cols],
            sent_sem.at[0], frecv_sem.at[which], sibling,
        )

    def arrived(part, sem):
        return remote(part, part, sent_sem.at[0], sem, sibling)

    def settle(which, a, blocks, cols=slice(None)):
        arrived(received[a].at[pl.ds(0, blocks * slot), cols], frecv_sem.at[which]).wait_recv()

    selects = [select_of(b) for b in range(groups)]
    chosen = jnp.concatenate([s.astype(f32) for s in selects], axis=0).astype(bf16)

    def store(a, cols, block):
        for b in range(groups):
            piece = block[b * slot : (b + 1) * slot]
            if b:
                packed[a][b - 1, :, cols] = piece
            else:
                received[a][rows(0, 0), cols] = piece

    for n, (start, size) in enumerate(pieces):
        loads[n].wait()
        cols = pl.ds(start, size)
        store(0, cols, mm(chosen, tok[:, cols], ((1,), (0,))).astype(bf16))
        if n == 0:
            entered = 1 + 2 * (half - 1) + 1
            if relayed:

                @pl.when(odd)
                def _():
                    pl.semaphore_wait(barrier, entered + 1)

                @pl.when(even)
                def _():
                    pl.semaphore_wait(barrier, entered)
            else:
                pl.semaphore_wait(barrier, entered)
        for c, (at, extent) in enumerate(spans(width, FIRST_X)):
            if at + extent == start + size:
                if c < lends:
                    go_first(c)
                for b in beside:
                    send(b, 0, c).start()
        if n == 0:
            for j in range(1, half):
                signal(ready_sem, device(wide, peer(j)))
    pl.when(jnp.logical_not(held_back))(go_more)
    for name in ("wgu", "wdn", "sm"):
        loads[name].start()
    loads["rw"].wait()
    loads["og"].wait()
    weights = rw[...]
    weight = jnp.concatenate(
        [jnp.sum(jnp.where(s, weights, 0.0), axis=1, keepdims=True) for s in selects], axis=0
    )
    for start, size in spans(width, PACK):
        cols = pl.ds(start, size)
        placed = mm(chosen, og[:, cols], ((1,), (0,)))
        store(1, cols, (weight * placed).astype(bf16))
    for b in beside:
        for c in range(len(parts[b, 1])):
            send(b, 1, c).start()
    if half > 1:
        pl.semaphore_wait(ready_sem, half - 1)
    if relayed:
        pl.when(jnp.logical_not(held_back))(go_rest)
    else:
        go_rest()
    for a in (0, 1):
        forward(0, a, slice(None), a).start()
    if relayed:

        @pl.when(even)
        def _():
            for c in range(lends):
                lend(c).wait_recv()
                hand_on(c).start()

    def project(r):
        projected = mm(rx[r, :], wgu[...], ((1,), (0,)))
        gate_pre = projected[:, :hidden_units]
        up_pre = projected[:, hidden_units:]
        logistic = jax.nn.sigmoid(gate_pre)
        swished = gate_pre * logistic
        hid[r, :] = (swished * up_pre).astype(bf16)
        return up_pre * logistic * (1.0 + gate_pre * (1.0 - logistic)), swished

    def finish(target, r, hidden_grad, factors):
        target[r, :] = jnp.concatenate(
            [hidden_grad * factors[0], hidden_grad * factors[1]], axis=1
        ).astype(bf16)

    def take(b, a, c, which):
        cols = cols_of(b, a, c)
        i = index[near if b == direct and a and which > 2 else b, a, c]
        arrived(received[a].at[rows(b, 0, swapped), cols], recv_sem.at[i]).wait_recv()
        forward(b, a, cols, which).start()

    def take_whole(b, a, which):
        i = index[direct if b == near and a else b, a, 0]
        arrived(received[a].at[rows(b, 0, swapped)], recv_sem.at[i]).wait_recv()
        forward(b, a, slice(None), which).start()

    for c in range(len(FIRST_X)):
        take(direct, 0, c, 0)
        if relayed and c < 2:
            ready = leads if c else jnp.logical_not(leads)
            pl.when(jnp.logical_and(held_back, ready))(go_rest)
    for b in beside:
        take_whole(b, 0, 0)
    settle(0, 0, half + 1)
    pl.when(far)(go_direct)
    pair = 2 * slot
    first, last = pl.ds(0, half * pair), pl.ds(half * pair, half * pair)
    soon, rest_rows = pl.ds(0, (half + 1) * pair), pl.ds((half + 1) * pair, (half - 1) * pair)
    for name in ("wgu", "wdn", "sm"):
        loads[name].wait()
    factors_soon = project(soon)
    factors_first = [factor[: half * pair] for factor in factors_soon]
    factors = [factor[half * pair :] for factor in factors_soon]
    for b in early[2:]:
        take_whole(b, 1, 1)

    @pl.when(jnp.logical_not(swapped))
    def _():
        take_whole(direct, 1, 1)

    @pl.when(swapped)
    def _():
        take_whole(near, 1, 1)

    moment[...] = (0.95 / second_correction) * sm[...].astype(f32)
    decay[...] = 0.1 * wdn[...].astype(f32)
    turned_wdn[...] = wdn[...].T
    settle(1, 1, half)
    finish(pre, first, mm(rd[first, :], wdn[...], ((1,), (1,))), factors_first)
    for i in range(width // 256):
        cols = pl.ds(i * 256, 256)
        acc_p[cols, :] = mm(rx[first, cols], pre[first, :], ((0,), (0,)))
        acc_d[:, cols] = mm(hid[first, :], rd[first, cols], ((0,), (0,)))
    for b in diagonal:
        for c in range(len(DIAGONAL_X)):
            take(b, 0, c, 2)

    def relay(c):
        for b in diagonal:
            take(b, 1, c, 3 + c)

        @pl.when(jnp.logical_not(swapped))
        def _():
            take(near, 1, c, 3 + c)

        @pl.when(swapped)
        def _():
            take(direct, 1, c, 3 + c)

    @pl.when(leads)
    def _():
        for c in range(final - 1):
            relay(c)

    settle(2, 0, half - 1)
    if half > 1:
        factors = [
            jnp.concatenate(both, axis=0) for both in zip(factors, project(rest_rows), strict=True)
        ]
    turned_hid = hid[last, :].T

    @pl.when(leads)
    def _():
        relay(final - 1)

    hidden_grad = jnp.zeros((half * 2 * slot, hidden_units), f32)
    late_d = spans(width, LATE_D)

    def add(c):
        cols = pl.ds(*late_d[c])
        return hidden_grad + mm(rd[last, cols], turned_wdn[cols, :], ((1,), (0,)))

    def update(c):
        cols = pl.ds(*late_d[c])
        total = acc_d[:, cols] + mm(turned_hid, rd[last, cols], ((1,), (0,)))
        second = moment[:, cols] + (0.05 / second_correction) * total * total
        root = second * lax.rsqrt(second)
        ustage[:, cols] = (total / (root + 1e-08) + decay[:, cols]).astype(bf16)

    follows = jnp.logical_not(leads)
    if AHEAD:
        pl.when(follows)(lambda: relay(0))
    for c in range(final):
        if c + AHEAD < final:
            pl.when(follows)(lambda c=c: relay(c + AHEAD))

        settle(3 + c, 1, half, pl.ds(*late_d[c]))
        hidden_grad = add(c)
        if c + 1 == final:
            finish(pre_last, slice(None), hidden_grad, factors)
        update(c)
        if c == TURN:
            turned[...] = rx[last, :].T

    def sent(part):
        arrived(part, recv_sem.at[0]).wait_send()

    sent(px)
    sent(pd)
    sent(rx.at[pl.ds(0, groups * slot)])
    sent(rd.at[pl.ds(0, groups * slot)])
    if relayed:
        pl.when(even)(lambda: sent(lent.at[:, pl.ds(0, first_columns)]))


def final_kernel(acc_p, turned, pre_last, update, gout, uout, gstage, out_sem):
    tiles = acc_p.shape[0] // 256
    outs = [pltpu.make_async_copy(update, uout.at[0], out_sem.at[0])]
    outs[0].start()
    for i in range(tiles):
        r = pl.ds(i * 256, 256)
        gstage[r, :] = (acc_p[r, :] + mm(turned[r, :], pre_last[...], ((1,), (0,)))).astype(bf16)
        copy = pltpu.make_async_copy(gstage.at[r], gout.at[0, r], out_sem.at[0])
        copy.start()
        outs.append(copy)
    for copy in outs:
        copy.wait()


def body(tokens, expert_ids, route_weights, out_grad, w_gate_up, w_down, second_moment):
    groups = lax.axis_size("narrow")
    wides = lax.axis_size("wide")
    count, width = tokens.shape
    cap = 3 * count // (2 * groups)
    slot = -(-cap // 16) * 16
    columns = w_gate_up.shape[2]
    units = w_down.shape[1]
    half = groups // 2
    all_rows = groups * 2 * slot
    last_rows = half * 2 * slot
    relayed = wides % 2 == 0 and wides >= 4
    chunks = len(FIRST_X) + half + half - 1 + (half - 1) * len(DIAGONAL_X) + half * len(LATE_D)
    dma = pltpu.SemaphoreType.DMA
    any_spec = pl.BlockSpec(memory_space=pl.ANY)
    vmem_spec = pl.BlockSpec(memory_space=pltpu.VMEM)
    held = pl.pallas_call(
        functools.partial(kernel, groups, wides, slot, relayed),
        out_shape=(
            pltpu.VMEM((width, columns), f32),
            pltpu.VMEM((width, last_rows), bf16),
            pltpu.VMEM((last_rows, columns), bf16),
            pltpu.VMEM((units, width), bf16),
        ),
        in_specs=[any_spec] * 7,
        out_specs=(vmem_spec,) * 4,
        scratch_shapes=[
            pltpu.VMEM((1, count), jnp.int32),
            pltpu.VMEM((1, count), f32),
            pltpu.VMEM((count, width), bf16),
            pltpu.VMEM((count, width), bf16),
            pltpu.VMEM((width, columns), bf16),
            pltpu.VMEM((units, width), bf16),
            pltpu.VMEM((units, width), bf16),
            pltpu.VMEM((groups - 1, slot, width), bf16),
            pltpu.VMEM((groups - 1, slot, width), bf16),
            pltpu.VMEM((all_rows, width), bf16),
            pltpu.VMEM((all_rows, width), bf16),
            pltpu.VMEM((slot, width), bf16),
            pltpu.VMEM((last_rows, columns), bf16),
            pltpu.VMEM((all_rows, units), bf16),
            pltpu.VMEM((units, width), f32),
            pltpu.VMEM((units, width), f32),
            pltpu.VMEM((units, width), f32),
            pltpu.VMEM((width, units), bf16),
            dma((6 + len(PACK),)), dma((1,)), dma((chunks,)), dma((max(LENDS, 1),)),
            dma((3 + len(LATE_D),)), pltpu.SemaphoreType.REGULAR,
        ],
        compiler_params=pltpu.CompilerParams(
            collective_id=0, has_side_effects=True, vmem_limit_bytes=LIMIT
        ),
    )(
        *(
            pltpu.with_memory_space_constraint(value, pltpu.HBM)
            for value in (
                expert_ids.reshape(1, count), route_weights.reshape(1, count),
                tokens, out_grad, w_gate_up, w_down, second_moment,
            )
        ),
    )
    return pl.pallas_call(
        final_kernel,
        out_shape=(
            jax.ShapeDtypeStruct((1, width, columns), bf16),
            jax.ShapeDtypeStruct((1, units, width), bf16),
        ),
        in_specs=[vmem_spec] * 4,
        out_specs=(any_spec, any_spec),
        scratch_shapes=[pltpu.VMEM((width, columns), bf16), dma((1,))],
        compiler_params=pltpu.CompilerParams(vmem_limit_bytes=LIMIT),
    )(*held)


def solution(mesh):
    placed = (
        P(("wide", "narrow"), None),
        P(("wide", "narrow")),
        P(("wide", "narrow")),
        P(("wide", "narrow"), None),
        P(("wide", "narrow"), None, None),
        P(("wide", "narrow"), None, None),
        P(("wide", "narrow"), None, None),
    )
    return jax.shard_map(
        body,
        mesh=mesh,
        in_specs=placed,
        out_specs=(P(("wide", "narrow"), None, None), P(("wide", "narrow"), None, None)),
        check_vma=False,
    )
```

```python
import functools

import jax
import jax.numpy as jnp
from jax import lax
from jax.experimental import pallas as pl
from jax.experimental.pallas import tpu as pltpu
from jax.sharding import PartitionSpec as P

second_correction = 1.0 - 0.95**10
bf16 = jnp.bfloat16
f32 = jnp.float32
LIMIT = 32 * 1024 * 1024


def mm(a, b, dims):
    return lax.dot_general(a, b, (dims, ((), ())), preferred_element_type=f32)


LENDS = 2
AHEAD = 1
TURN = 1
PACK = (2, 3, 3)
FIRST_X = (2, 3, 3)
EARLY_D = (5, 3)
DIAGONAL_X = (4, 2, 2)
LATE_D = (3, 2, 2, 1)


def spans(width, weights):
    unit = width // sum(weights)
    out, at = [], 0
    for weight in weights:
        out.append((at * unit, weight * unit))
        at += weight
    return out


def kernel(
    groups, wides, slot, relayed,
    ids_hbm, rw_hbm, tok_hbm, og_hbm, wgu_hbm, wdn_hbm, sm_hbm,
    acc_p, turned, pre_last, ustage,
    ids, rw, tok, og, wgu, wdn, sm, px, pd, rx, rd, lent, pre, hid, acc_d, moment, decay, turned_wdn,
    in_sem, sent_sem, recv_sem, lent_sem, frecv_sem, ready_sem, pair_sem,
):
    half = groups // 2
    width = tok.shape[1]
    hidden_units = wdn.shape[0]
    wide = lax.axis_index("wide")
    narrow = lax.axis_index("narrow")
    home = narrow // 2
    parity = lax.rem(narrow, 2)

    def along(step):
        return lax.rem(wide + wides + step, wides)

    def device(w, n):
        return {"wide": w, "narrow": n}

    def peer(j, other=0):
        return 2 * lax.rem(home + j, half) + lax.rem(parity + other, 2)

    def crossed(step, j):
        same = jnp.logical_and(along(step) == 0, lax.rem(home + j, half) == 0)
        return jnp.where(same, 0, 1)

    def target(step, j, a):
        return device(along(step), peer(j, crossed(step, j) if a else 0))

    odd = lax.rem(wide, 2) == 1
    even = jnp.logical_not(odd)
    sibling = device(wide, 2 * home + 1 - parity)
    leads = parity != crossed(0, 0)

    order = [(0, 0), (1, 0)] + [(0, j) for j in range(2, half)]
    order += [(0, 1)] + [(1, j) for j in range(1, half)]
    early = list(range(half))
    late = list(range(half, groups))
    direct = 1
    diagonal = [b for b in late if order[b][0]]
    beside = [b for b in range(1, groups) if not order[b][0]]

    pieces = spans(width, PACK)
    loads = {}

    def load(name, src, dst, i):
        loads[name] = pltpu.make_async_copy(src, dst, in_sem.at[i])

    load("ids", ids_hbm, ids, 0)
    for n, piece in enumerate(pieces):
        load(n, tok_hbm.at[:, pl.ds(*piece)], tok.at[:, pl.ds(*piece)], 6 + n)
    load("rw", rw_hbm, rw, 1)
    load("og", og_hbm, og, 2)
    for copy in loads.values():
        copy.start()
    load("wgu", wgu_hbm.at[0], wgu, 3)
    load("wdn", wdn_hbm.at[0], wdn, 4)
    load("sm", sm_hbm.at[0], sm, 5)

    barrier = pltpu.get_barrier_semaphore()

    def signal(sem, partner):
        pl.semaphore_signal(sem, inc=1, device_id=partner, device_id_type=pl.DeviceIdType.MESH)

    signal(barrier, device(along(-1), narrow))
    for j in range(1, half):
        signal(barrier, device(wide, peer(j)))
    signal(barrier, sibling)
    if relayed:

        @pl.when(even)
        def _():
            signal(barrier, device(along(1), narrow))

    loads["ids"].wait()
    count = tok.shape[0]
    labels = ids[...]
    pad_groups = max(8, groups)
    onehot = (lax.broadcasted_iota(jnp.int32, (pad_groups, count), 0) == labels).astype(f32)
    before = (
        lax.broadcasted_iota(jnp.int32, (count, count), 0)
        < lax.broadcasted_iota(jnp.int32, (count, count), 1)
    ).astype(f32)
    counted = mm(onehot.astype(bf16), before.astype(bf16), ((1,), (0,)))
    within = jnp.sum(counted * onehot, axis=0, keepdims=True).astype(jnp.int32)
    slots = lax.broadcasted_iota(jnp.int32, (slot, count), 0)

    def select_of(b):
        kind, j = order[b]
        value = kind * half + lax.rem(home + j, half)
        return jnp.logical_and(labels == value, slots == within)

    near = half
    far = jnp.logical_and(wide == wides - 1, home > 0)
    swapped = jnp.logical_and(wide == 0, home > 0)
    near_swapped = jnp.logical_and(wide == 0, lax.rem(home + 1, half) > 0)
    lent_swapped = jnp.logical_and(along(2) == 0, home > 0)

    def rows(b, h, swap):
        at = jnp.where(swap, direct + near - b, b) if b in (direct, near) else b
        start = (2 * at + h) * slot
        return pl.ds(start if isinstance(start, int) else pl.multiple_of(start, slot), slot)

    def remote(src, dst, s, r, dev):
        return pltpu.make_async_remote_copy(
            src_ref=src, dst_ref=dst, send_sem=s, recv_sem=r,
            device_id=dev, device_id_type=pl.DeviceIdType.MESH,
        )

    index, parts, used = {}, {}, 0
    for b in range(1, groups):
        widths = (DIAGONAL_X if b in diagonal else FIRST_X, EARLY_D if b in early[2:] else LATE_D)
        for a in (0, 1):
            parts[b, a] = spans(width, widths[a])
            one = b in beside if a == 0 else b in early
            for c in range(len(parts[b, a])):
                index[b, a, c] = used if one else used + c
            used += 1 if one else len(parts[b, a])

    packed, received = (px, pd), (rx, rd)

    def cols_of(b, a, c):
        return pl.ds(*parts[b, a][c])

    def slot_of(b, a, c, swap):
        if a and b in (direct, near):
            return jnp.where(swap, index[direct + near - b, 1, c], index[b, 1, c])
        return index[b, a, c]

    def send(b, a, c):
        kind, j = order[b]
        cols, swap = cols_of(b, a, c), far if b == direct else near_swapped
        return remote(
            packed[a].at[b - 1, :, cols],
            received[a].at[rows(b, crossed(kind, j) if a else 0, swap), cols],
            sent_sem.at[0], recv_sem.at[slot_of(b, a, c, swap)], target(kind, j, a),
        )

    lends = LENDS if relayed else 0

    def lend(c):
        cols = cols_of(direct, 0, c)
        return remote(
            px.at[direct - 1, :, cols], lent.at[:, cols],
            sent_sem.at[0], lent_sem.at[c], device(along(-1), narrow),
        )

    def hand_on(c):
        cols = cols_of(direct, 0, c)
        return remote(
            lent.at[:, cols], rx.at[rows(direct, 0, lent_swapped), cols],
            sent_sem.at[0], recv_sem.at[index[direct, 0, c]], target(2, 0, 0),
        )

    def go_first(c):
        if relayed:

            @pl.when(odd)
            def _():
                lend(c).start()

            @pl.when(even)
            def _():
                send(direct, 0, c).start()
        else:
            send(direct, 0, c).start()

    def go_direct():
        for c in range(len(parts[direct, 1])):
            send(direct, 1, c).start()

    def go_more():
        for c in range(lends, len(FIRST_X)):
            send(direct, 0, c).start()

    held_back = jnp.logical_and(odd, wide != wides - 1) if relayed else wide < 0

    def go_rest():
        pl.when(held_back)(go_more)
        pl.when(jnp.logical_not(far))(go_direct)
        for a in (0, 1):
            for b in diagonal:
                for c in range(len(parts[b, a])):
                    send(b, a, c).start()

    first_columns = sum(FIRST_X[:lends]) * width // sum(FIRST_X)

    final = len(LATE_D)

    def heard(b, a):
        return crossed(0, 0) if a and b else 0

    def forward(b, a, cols, which):
        h = heard(b, a)
        return remote(
            received[a].at[rows(b, h, swapped), cols],
            received[a].at[rows(b, 1 - h, swapped), cols],
            sent_sem.at[0], frecv_sem.at[which], sibling,
        )

    def arrived(part, sem):
        return remote(part, part, sent_sem.at[0], sem, sibling)

    def settle(which, a, blocks, cols=slice(None)):
        arrived(received[a].at[pl.ds(0, blocks * slot), cols], frecv_sem.at[which]).wait_recv()

    selects = [select_of(b) for b in range(groups)]
    chosen = jnp.concatenate([s.astype(f32) for s in selects], axis=0).astype(bf16)

    def store(a, cols, block):
        for b in range(groups):
            piece = block[b * slot : (b + 1) * slot]
            if b:
                packed[a][b - 1, :, cols] = piece
            else:
                received[a][rows(0, 0, swapped), cols] = piece

    for n, (start, size) in enumerate(pieces):
        loads[n].wait()
        cols = pl.ds(start, size)
        store(0, cols, mm(chosen, tok[:, cols], ((1,), (0,))).astype(bf16))
        if n == 0:
            entered = 1 + half - 1 + 1
            if relayed:

                @pl.when(odd)
                def _():
                    pl.semaphore_wait(barrier, entered + 1)

                @pl.when(even)
                def _():
                    pl.semaphore_wait(barrier, entered)
            else:
                pl.semaphore_wait(barrier, entered)
        for c, (at, extent) in enumerate(spans(width, FIRST_X)):
            if at + extent == start + size:
                if c < lends:
                    go_first(c)
                for b in beside:
                    send(b, 0, c).start()
        if n == 0:
            for j in range(1, half):
                signal(ready_sem, device(wide, peer(j)))
    pl.when(jnp.logical_not(held_back))(go_more)
    for name in ("wgu", "wdn", "sm"):
        loads[name].start()
    loads["rw"].wait()
    loads["og"].wait()
    weights = rw[...]
    weight = jnp.concatenate(
        [jnp.sum(jnp.where(s, weights, 0.0), axis=1, keepdims=True) for s in selects], axis=0
    )
    for start, size in spans(width, PACK):
        cols = pl.ds(start, size)
        placed = mm(chosen, og[:, cols], ((1,), (0,)))
        store(1, cols, (weight * placed).astype(bf16))
    if half > 1:
        pl.semaphore_wait(ready_sem, half - 1)
    signal(pair_sem, sibling)
    pl.semaphore_wait(pair_sem, 1)
    for b in beside:
        for c in range(len(parts[b, 1])):
            send(b, 1, c).start()
    if relayed:
        pl.when(jnp.logical_not(held_back))(go_rest)
    else:
        go_rest()
    for a in (0, 1):
        forward(0, a, slice(None), a).start()
    if relayed:

        @pl.when(even)
        def _():
            for c in range(lends):
                lend(c).wait_recv()
                hand_on(c).start()

    def project(r):
        projected = mm(rx[r, :], wgu[...], ((1,), (0,)))
        gate_pre = projected[:, :hidden_units]
        up_pre = projected[:, hidden_units:]
        logistic = jax.nn.sigmoid(gate_pre)
        swished = gate_pre * logistic
        hid[r, :] = (swished * up_pre).astype(bf16)
        return up_pre * logistic * (1.0 + gate_pre * (1.0 - logistic)), swished

    def finish(target, r, hidden_grad, factors):
        target[r, :] = jnp.concatenate(
            [hidden_grad * factors[0], hidden_grad * factors[1]], axis=1
        ).astype(bf16)

    def take(b, a, c, which):
        cols = cols_of(b, a, c)
        i = index[near if b == direct and a and which > 2 else b, a, c]
        arrived(received[a].at[rows(b, heard(b, a), swapped), cols], recv_sem.at[i]).wait_recv()
        forward(b, a, cols, which).start()

    def take_whole(b, a, which):
        i = index[direct if b == near and a else b, a, 0]
        arrived(received[a].at[rows(b, heard(b, a), swapped)], recv_sem.at[i]).wait_recv()
        forward(b, a, slice(None), which).start()

    for c in range(len(FIRST_X)):
        take(direct, 0, c, 0)
        if relayed and c < 2:
            pl.when(jnp.logical_and(held_back, parity == c))(go_rest)
    for b in beside:
        take_whole(b, 0, 0)
    settle(0, 0, half + 1)
    pl.when(far)(go_direct)
    pair = 2 * slot
    first, last = pl.ds(0, half * pair), pl.ds(half * pair, half * pair)
    soon, rest_rows = pl.ds(0, (half + 1) * pair), pl.ds((half + 1) * pair, (half - 1) * pair)
    for name in ("wgu", "wdn", "sm"):
        loads[name].wait()
    factors_soon = project(soon)
    factors_first = [factor[: half * pair] for factor in factors_soon]
    factors = [factor[half * pair :] for factor in factors_soon]
    for b in early[2:]:
        take_whole(b, 1, 1)

    @pl.when(jnp.logical_not(swapped))
    def _():
        take_whole(direct, 1, 1)

    @pl.when(swapped)
    def _():
        take_whole(near, 1, 1)

    moment[...] = (0.95 / second_correction) * sm[...].astype(f32)
    decay[...] = 0.1 * wdn[...].astype(f32)
    turned_wdn[...] = wdn[...].T
    settle(1, 1, half)
    finish(pre, first, mm(rd[first, :], wdn[...], ((1,), (1,))), factors_first)
    for i in range(width // 256):
        cols = pl.ds(i * 256, 256)
        acc_p[cols, :] = mm(rx[first, cols], pre[first, :], ((0,), (0,)))
        acc_d[:, cols] = mm(hid[first, :], rd[first, cols], ((0,), (0,)))
    for b in diagonal:
        for c in range(len(DIAGONAL_X)):
            take(b, 0, c, 2)

    def relay(c):
        for b in diagonal:
            take(b, 1, c, 3 + c)

        @pl.when(jnp.logical_not(swapped))
        def _():
            take(near, 1, c, 3 + c)

        @pl.when(swapped)
        def _():
            take(direct, 1, c, 3 + c)

    @pl.when(leads)
    def _():
        for c in range(final - 1):
            relay(c)

    settle(2, 0, half - 1)
    if half > 1:
        factors = [
            jnp.concatenate(both, axis=0) for both in zip(factors, project(rest_rows), strict=True)
        ]
    turned_hid = hid[last, :].T

    @pl.when(leads)
    def _():
        relay(final - 1)

    hidden_grad = jnp.zeros((half * 2 * slot, hidden_units), f32)
    late_d = spans(width, LATE_D)

    def add(c):
        cols = pl.ds(*late_d[c])
        return hidden_grad + mm(rd[last, cols], turned_wdn[cols, :], ((1,), (0,)))

    def update(c):
        cols = pl.ds(*late_d[c])
        total = acc_d[:, cols] + mm(turned_hid, rd[last, cols], ((1,), (0,)))
        second = moment[:, cols] + (0.05 / second_correction) * total * total
        root = second * lax.rsqrt(second)
        ustage[:, cols] = (total / (root + 1e-08) + decay[:, cols]).astype(bf16)

    follows = jnp.logical_not(leads)
    if AHEAD:
        pl.when(follows)(lambda: relay(0))
    for c in range(final):
        if c + AHEAD < final:
            pl.when(follows)(lambda c=c: relay(c + AHEAD))

        settle(3 + c, 1, half, pl.ds(*late_d[c]))
        hidden_grad = add(c)
        if c + 1 == final:
            finish(pre_last, slice(None), hidden_grad, factors)
        update(c)
        if c == TURN:
            turned[...] = rx[last, :].T

    def sent(part):
        arrived(part, recv_sem.at[0]).wait_send()

    sent(px)
    sent(pd)
    sent(rx.at[pl.ds(0, groups * slot)])
    sent(rd.at[pl.ds(0, groups * slot)])
    if relayed:
        pl.when(even)(lambda: sent(lent.at[:, pl.ds(0, first_columns)]))


def final_kernel(acc_p, turned, pre_last, update, gout, uout, gstage, out_sem):
    tiles = acc_p.shape[0] // 256
    outs = [pltpu.make_async_copy(update, uout.at[0], out_sem.at[0])]
    outs[0].start()
    for i in range(tiles):
        r = pl.ds(i * 256, 256)
        gstage[r, :] = (acc_p[r, :] + mm(turned[r, :], pre_last[...], ((1,), (0,)))).astype(bf16)
        copy = pltpu.make_async_copy(gstage.at[r], gout.at[0, r], out_sem.at[0])
        copy.start()
        outs.append(copy)
    for copy in outs:
        copy.wait()


def body(tokens, expert_ids, route_weights, out_grad, w_gate_up, w_down, second_moment):
    groups = lax.axis_size("narrow")
    wides = lax.axis_size("wide")
    count, width = tokens.shape
    cap = 3 * count // (2 * groups)
    slot = -(-cap // 16) * 16
    columns = w_gate_up.shape[2]
    units = w_down.shape[1]
    half = groups // 2
    all_rows = groups * 2 * slot
    last_rows = half * 2 * slot
    relayed = wides % 2 == 0 and wides >= 4
    chunks = len(FIRST_X) + half + half - 1 + (half - 1) * len(DIAGONAL_X) + half * len(LATE_D)
    dma = pltpu.SemaphoreType.DMA
    any_spec = pl.BlockSpec(memory_space=pl.ANY)
    vmem_spec = pl.BlockSpec(memory_space=pltpu.VMEM)
    held = pl.pallas_call(
        functools.partial(kernel, groups, wides, slot, relayed),
        out_shape=(
            pltpu.VMEM((width, columns), f32),
            pltpu.VMEM((width, last_rows), bf16),
            pltpu.VMEM((last_rows, columns), bf16),
            pltpu.VMEM((units, width), bf16),
        ),
        in_specs=[any_spec] * 7,
        out_specs=(vmem_spec,) * 4,
        scratch_shapes=[
            pltpu.VMEM((1, count), jnp.int32),
            pltpu.VMEM((1, count), f32),
            pltpu.VMEM((count, width), bf16),
            pltpu.VMEM((count, width), bf16),
            pltpu.VMEM((width, columns), bf16),
            pltpu.VMEM((units, width), bf16),
            pltpu.VMEM((units, width), bf16),
            pltpu.VMEM((groups - 1, slot, width), bf16),
            pltpu.VMEM((groups - 1, slot, width), bf16),
            pltpu.VMEM((all_rows, width), bf16),
            pltpu.VMEM((all_rows, width), bf16),
            pltpu.VMEM((slot, width), bf16),
            pltpu.VMEM((last_rows, columns), bf16),
            pltpu.VMEM((all_rows, units), bf16),
            pltpu.VMEM((units, width), f32),
            pltpu.VMEM((units, width), f32),
            pltpu.VMEM((units, width), f32),
            pltpu.VMEM((width, units), bf16),
            dma((6 + len(PACK),)), dma((1,)), dma((chunks,)), dma((max(LENDS, 1),)),
            dma((3 + len(LATE_D),)), pltpu.SemaphoreType.REGULAR, pltpu.SemaphoreType.REGULAR,
        ],
        compiler_params=pltpu.CompilerParams(
            collective_id=0, has_side_effects=True, vmem_limit_bytes=LIMIT
        ),
    )(
        *(
            pltpu.with_memory_space_constraint(value, pltpu.HBM)
            for value in (
                expert_ids.reshape(1, count), route_weights.reshape(1, count),
                tokens, out_grad, w_gate_up, w_down, second_moment,
            )
        ),
    )
    return pl.pallas_call(
        final_kernel,
        out_shape=(
            jax.ShapeDtypeStruct((1, width, columns), bf16),
            jax.ShapeDtypeStruct((1, units, width), bf16),
        ),
        in_specs=[vmem_spec] * 4,
        out_specs=(any_spec, any_spec),
        scratch_shapes=[pltpu.VMEM((width, columns), bf16), dma((1,))],
        compiler_params=pltpu.CompilerParams(vmem_limit_bytes=LIMIT),
    )(*held)


def solution(mesh):
    placed = (
        P(("wide", "narrow"), None),
        P(("wide", "narrow")),
        P(("wide", "narrow")),
        P(("wide", "narrow"), None),
        P(("wide", "narrow"), None, None),
        P(("wide", "narrow"), None, None),
        P(("wide", "narrow"), None, None),
    )
    return jax.shard_map(
        body,
        mesh=mesh,
        in_specs=placed,
        out_specs=(P(("wide", "narrow"), None, None), P(("wide", "narrow"), None, None)),
        check_vma=False,
    )
```

```python
import functools

import jax
import jax.numpy as jnp
from jax import lax
from jax.experimental import pallas as pl
from jax.experimental.pallas import tpu as pltpu
from jax.sharding import PartitionSpec as P

second_correction = 1.0 - 0.95**10
bf16 = jnp.bfloat16
f32 = jnp.float32
LIMIT = 32 * 1024 * 1024


def mm(a, b, dims):
    return lax.dot_general(a, b, (dims, ((), ())), preferred_element_type=f32)


LENDS = 2
AHEAD = 2
TURN = 1
PACK = (2, 3, 3)
FIRST_X = (2, 3, 3)
EARLY_D = (5, 3)
DIAGONAL_X = (4, 4)
LATE_D = (3, 2, 2, 1)


def spans(width, weights):
    unit = width // sum(weights)
    out, at = [], 0
    for weight in weights:
        out.append((at * unit, weight * unit))
        at += weight
    return out


def kernel(
    groups, wides, slot, relayed,
    ids_hbm, rw_hbm, tok_hbm, og_hbm, wgu_hbm, wdn_hbm, sm_hbm,
    acc_p, turned, pre_last, ustage,
    ids, rw, tok, og, wgu, wdn, sm, px, pd, rx, rd, lent, pre, hid, acc_d, moment, decay, turned_wdn,
    in_sem, sent_sem, recv_sem, lent_sem, frecv_sem, ready_sem, pair_sem,
):
    half = groups // 2
    width = tok.shape[1]
    hidden_units = wdn.shape[0]
    wide = lax.axis_index("wide")
    narrow = lax.axis_index("narrow")
    home = narrow // 2
    parity = lax.rem(narrow, 2)

    def along(step):
        return lax.rem(wide + wides + step, wides)

    def device(w, n):
        return {"wide": w, "narrow": n}

    def peer(j, other=0):
        return 2 * lax.rem(home + j, half) + lax.rem(parity + other, 2)

    def crossed(step, j):
        same = jnp.logical_and(along(step) == 0, lax.rem(home + j, half) == 0)
        return jnp.where(same, 0, 1)

    def target(step, j, a):
        return device(along(step), peer(j, crossed(step, j) if a else 0))

    odd = lax.rem(wide, 2) == 1
    even = jnp.logical_not(odd)
    sibling = device(wide, 2 * home + 1 - parity)
    leads = parity != crossed(0, 0)

    order = [(0, 0), (1, 0)] + [(0, j) for j in range(2, half)]
    order += [(0, 1)] + [(1, j) for j in range(1, half)]
    early = list(range(half))
    late = list(range(half, groups))
    direct = 1
    diagonal = [b for b in late if order[b][0]]
    beside = [b for b in range(1, groups) if not order[b][0]]

    pieces = spans(width, PACK)
    loads = {}

    def load(name, src, dst, i):
        loads[name] = pltpu.make_async_copy(src, dst, in_sem.at[i])

    load("ids", ids_hbm, ids, 0)
    for n, piece in enumerate(pieces):
        load(n, tok_hbm.at[:, pl.ds(*piece)], tok.at[:, pl.ds(*piece)], 6 + n)
    load("rw", rw_hbm, rw, 1)
    load("og", og_hbm, og, 2)
    for copy in loads.values():
        copy.start()
    load("wgu", wgu_hbm.at[0], wgu, 3)
    load("wdn", wdn_hbm.at[0], wdn, 4)
    load("sm", sm_hbm.at[0], sm, 5)

    barrier = pltpu.get_barrier_semaphore()

    def signal(sem, partner):
        pl.semaphore_signal(sem, inc=1, device_id=partner, device_id_type=pl.DeviceIdType.MESH)

    signal(barrier, device(along(-1), narrow))
    for j in range(1, half):
        signal(barrier, device(wide, peer(j)))
    signal(barrier, sibling)
    if relayed:

        @pl.when(even)
        def _():
            signal(barrier, device(along(1), narrow))

    loads["ids"].wait()
    count = tok.shape[0]
    labels = ids[...]
    pad_groups = max(8, groups)
    onehot = (lax.broadcasted_iota(jnp.int32, (pad_groups, count), 0) == labels).astype(f32)
    before = (
        lax.broadcasted_iota(jnp.int32, (count, count), 0)
        < lax.broadcasted_iota(jnp.int32, (count, count), 1)
    ).astype(f32)
    counted = mm(onehot.astype(bf16), before.astype(bf16), ((1,), (0,)))
    within = jnp.sum(counted * onehot, axis=0, keepdims=True).astype(jnp.int32)
    slots = lax.broadcasted_iota(jnp.int32, (slot, count), 0)

    def select_of(b):
        kind, j = order[b]
        value = kind * half + lax.rem(home + j, half)
        return jnp.logical_and(labels == value, slots == within)

    near = half
    far = jnp.logical_and(wide == wides - 1, home > 0)
    swapped = jnp.logical_and(wide == 0, home > 0)
    near_swapped = jnp.logical_and(wide == 0, lax.rem(home + 1, half) > 0)
    lent_swapped = jnp.logical_and(along(2) == 0, home > 0)

    def rows(b, h, swap):
        at = jnp.where(swap, direct + near - b, b) if b in (direct, near) else b
        start = (2 * at + h) * slot
        return pl.ds(start if isinstance(start, int) else pl.multiple_of(start, slot), slot)

    def remote(src, dst, s, r, dev):
        return pltpu.make_async_remote_copy(
            src_ref=src, dst_ref=dst, send_sem=s, recv_sem=r,
            device_id=dev, device_id_type=pl.DeviceIdType.MESH,
        )

    index, parts, used = {}, {}, 0
    for b in range(1, groups):
        widths = (DIAGONAL_X if b in diagonal else FIRST_X, EARLY_D if b in early[2:] else LATE_D)
        for a in (0, 1):
            parts[b, a] = spans(width, widths[a])
            one = b in beside if a == 0 else b in early
            for c in range(len(parts[b, a])):
                index[b, a, c] = used if one else used + c
            used += 1 if one else len(parts[b, a])

    packed, received = (px, pd), (rx, rd)

    def cols_of(b, a, c):
        return pl.ds(*parts[b, a][c])

    def slot_of(b, a, c, swap):
        if a and b in (direct, near):
            return jnp.where(swap, index[direct + near - b, 1, c], index[b, 1, c])
        return index[b, a, c]

    def send(b, a, c):
        kind, j = order[b]
        cols, swap = cols_of(b, a, c), far if b == direct else near_swapped
        return remote(
            packed[a].at[b - 1, :, cols],
            received[a].at[rows(b, crossed(kind, j) if a else 0, swap), cols],
            sent_sem.at[0], recv_sem.at[slot_of(b, a, c, swap)], target(kind, j, a),
        )

    lends = LENDS if relayed else 0

    def lend(c):
        cols = cols_of(direct, 0, c)
        return remote(
            px.at[direct - 1, :, cols], lent.at[:, cols],
            sent_sem.at[0], lent_sem.at[c], device(along(-1), narrow),
        )

    def hand_on(c):
        cols = cols_of(direct, 0, c)
        return remote(
            lent.at[:, cols], rx.at[rows(direct, 0, lent_swapped), cols],
            sent_sem.at[0], recv_sem.at[index[direct, 0, c]], target(2, 0, 0),
        )

    def go_first(c):
        if relayed:

            @pl.when(odd)
            def _():
                lend(c).start()

            @pl.when(even)
            def _():
                send(direct, 0, c).start()
        else:
            send(direct, 0, c).start()

    def go_direct():
        for c in range(len(parts[direct, 1])):
            send(direct, 1, c).start()

    def go_more():
        for c in range(lends, len(FIRST_X)):
            send(direct, 0, c).start()

    held_back = jnp.logical_and(odd, wide != wides - 1) if relayed else wide < 0

    def go_rest():
        pl.when(held_back)(go_more)
        pl.when(jnp.logical_not(far))(go_direct)
        for a in (0, 1):
            for b in diagonal:
                for c in range(len(parts[b, a])):
                    send(b, a, c).start()

    first_columns = sum(FIRST_X[:lends]) * width // sum(FIRST_X)

    final = len(LATE_D)

    def heard(b, a):
        return crossed(0, 0) if a and b else 0

    def forward(b, a, cols, which):
        h = heard(b, a)
        return remote(
            received[a].at[rows(b, h, swapped), cols],
            received[a].at[rows(b, 1 - h, swapped), cols],
            sent_sem.at[0], frecv_sem.at[which], sibling,
        )

    def arrived(part, sem):
        return remote(part, part, sent_sem.at[0], sem, sibling)

    def settle(which, a, blocks, cols=slice(None)):
        arrived(received[a].at[pl.ds(0, blocks * slot), cols], frecv_sem.at[which]).wait_recv()

    selects = [select_of(b) for b in range(groups)]
    chosen = jnp.concatenate([s.astype(f32) for s in selects], axis=0).astype(bf16)

    def store(a, cols, block):
        for b in range(groups):
            piece = block[b * slot : (b + 1) * slot]
            if b:
                packed[a][b - 1, :, cols] = piece
            else:
                received[a][rows(0, 0, swapped), cols] = piece

    for n, (start, size) in enumerate(pieces):
        loads[n].wait()
        cols = pl.ds(start, size)
        store(0, cols, mm(chosen, tok[:, cols], ((1,), (0,))).astype(bf16))
        if n == 0:
            entered = 1 + half - 1 + 1
            if relayed:

                @pl.when(odd)
                def _():
                    pl.semaphore_wait(barrier, entered + 1)

                @pl.when(even)
                def _():
                    pl.semaphore_wait(barrier, entered)
            else:
                pl.semaphore_wait(barrier, entered)
        for c, (at, extent) in enumerate(spans(width, FIRST_X)):
            if at + extent == start + size:
                if c < lends:
                    go_first(c)
                for b in beside:
                    send(b, 0, c).start()
        if n == 0:
            for j in range(1, half):
                signal(ready_sem, device(wide, peer(j)))
    pl.when(jnp.logical_not(held_back))(go_more)
    for name in ("wgu", "wdn", "sm"):
        loads[name].start()
    loads["rw"].wait()
    loads["og"].wait()
    weights = rw[...]
    weight = jnp.concatenate(
        [jnp.sum(jnp.where(s, weights, 0.0), axis=1, keepdims=True) for s in selects], axis=0
    )
    for start, size in spans(width, PACK):
        cols = pl.ds(start, size)
        placed = mm(chosen, og[:, cols], ((1,), (0,)))
        store(1, cols, (weight * placed).astype(bf16))
    if half > 1:
        pl.semaphore_wait(ready_sem, half - 1)
    signal(pair_sem, sibling)
    pl.semaphore_wait(pair_sem, 1)
    for b in beside:
        for c in range(len(parts[b, 1])):
            send(b, 1, c).start()
    if relayed:
        pl.when(jnp.logical_not(held_back))(go_rest)
    else:
        go_rest()
    for a in (0, 1):
        forward(0, a, slice(None), a).start()
    if relayed:

        @pl.when(even)
        def _():
            for c in range(lends):
                lend(c).wait_recv()
                hand_on(c).start()

    def project(r):
        projected = mm(rx[r, :], wgu[...], ((1,), (0,)))
        gate_pre = projected[:, :hidden_units]
        up_pre = projected[:, hidden_units:]
        logistic = jax.nn.sigmoid(gate_pre)
        swished = gate_pre * logistic
        hid[r, :] = (swished * up_pre).astype(bf16)
        return up_pre * logistic * (1.0 + gate_pre * (1.0 - logistic)), swished

    def finish(target, r, hidden_grad, factors):
        target[r, :] = jnp.concatenate(
            [hidden_grad * factors[0], hidden_grad * factors[1]], axis=1
        ).astype(bf16)

    def take(b, a, c, which):
        cols = cols_of(b, a, c)
        i = index[near if b == direct and a and which > 2 else b, a, c]
        arrived(received[a].at[rows(b, heard(b, a), swapped), cols], recv_sem.at[i]).wait_recv()
        forward(b, a, cols, which).start()

    def take_whole(b, a, which):
        i = index[direct if b == near and a else b, a, 0]
        arrived(received[a].at[rows(b, heard(b, a), swapped)], recv_sem.at[i]).wait_recv()
        forward(b, a, slice(None), which).start()

    for c in range(len(FIRST_X)):
        take(direct, 0, c, 0)
        if relayed and c < 2:
            pl.when(jnp.logical_and(held_back, parity == c))(go_rest)
    for b in beside:
        take_whole(b, 0, 0)
    settle(0, 0, half + 1)
    pl.when(far)(go_direct)
    pair = 2 * slot
    first, last = pl.ds(0, half * pair), pl.ds(half * pair, half * pair)
    soon, rest_rows = pl.ds(0, (half + 1) * pair), pl.ds((half + 1) * pair, (half - 1) * pair)
    for name in ("wgu", "wdn", "sm"):
        loads[name].wait()
    factors_soon = project(soon)
    factors_first = [factor[: half * pair] for factor in factors_soon]
    factors = [factor[half * pair :] for factor in factors_soon]
    for b in early[2:]:
        take_whole(b, 1, 1)

    @pl.when(jnp.logical_not(swapped))
    def _():
        take_whole(direct, 1, 1)

    @pl.when(swapped)
    def _():
        take_whole(near, 1, 1)

    moment[...] = (0.95 / second_correction) * sm[...].astype(f32)
    decay[...] = 0.1 * wdn[...].astype(f32)
    turned_wdn[...] = wdn[...].T
    settle(1, 1, half)
    finish(pre, first, mm(rd[first, :], wdn[...], ((1,), (1,))), factors_first)
    for i in range(width // 256):
        cols = pl.ds(i * 256, 256)
        acc_p[cols, :] = mm(rx[first, cols], pre[first, :], ((0,), (0,)))
        acc_d[:, cols] = mm(hid[first, :], rd[first, cols], ((0,), (0,)))
    for b in diagonal:
        for c in range(len(DIAGONAL_X)):
            take(b, 0, c, 2)

    def relay(c):
        for b in diagonal:
            take(b, 1, c, 3 + c)

        @pl.when(jnp.logical_not(swapped))
        def _():
            take(near, 1, c, 3 + c)

        @pl.when(swapped)
        def _():
            take(direct, 1, c, 3 + c)

    @pl.when(leads)
    def _():
        for c in range(final - 1):
            relay(c)

    settle(2, 0, half - 1)
    if half > 1:
        factors = [
            jnp.concatenate(both, axis=0) for both in zip(factors, project(rest_rows), strict=True)
        ]
    turned_hid = hid[last, :].T

    @pl.when(leads)
    def _():
        relay(final - 1)

    hidden_grad = jnp.zeros((half * 2 * slot, hidden_units), f32)
    late_d = spans(width, LATE_D)

    def add(c):
        cols = pl.ds(*late_d[c])
        return hidden_grad + mm(rd[last, cols], turned_wdn[cols, :], ((1,), (0,)))

    def update(c):
        cols = pl.ds(*late_d[c])
        total = acc_d[:, cols] + mm(turned_hid, rd[last, cols], ((1,), (0,)))
        second = moment[:, cols] + (0.05 / second_correction) * total * total
        root = second * lax.rsqrt(second)
        ustage[:, cols] = (total / (root + 1e-08) + decay[:, cols]).astype(bf16)

    follows = jnp.logical_not(leads)
    for c in range(AHEAD):
        pl.when(follows)(lambda c=c: relay(c))
    for c in range(final):
        if c + AHEAD < final:
            pl.when(follows)(lambda c=c: relay(c + AHEAD))

        settle(3 + c, 1, half, pl.ds(*late_d[c]))
        hidden_grad = add(c)
        if c + 1 == final:
            finish(pre_last, slice(None), hidden_grad, factors)
        update(c)
        if c == TURN:
            turned[...] = rx[last, :].T

    def sent(part):
        arrived(part, recv_sem.at[0]).wait_send()

    sent(px)
    sent(pd)
    sent(rx.at[pl.ds(0, groups * slot)])
    sent(rd.at[pl.ds(0, groups * slot)])
    if relayed:
        pl.when(even)(lambda: sent(lent.at[:, pl.ds(0, first_columns)]))


def final_kernel(acc_p, turned, pre_last, update, gout, uout, gstage, out_sem):
    tiles = acc_p.shape[0] // 256
    outs = [pltpu.make_async_copy(update, uout.at[0], out_sem.at[0])]
    outs[0].start()
    for i in range(tiles):
        r = pl.ds(i * 256, 256)
        gstage[r, :] = (acc_p[r, :] + mm(turned[r, :], pre_last[...], ((1,), (0,)))).astype(bf16)
        copy = pltpu.make_async_copy(gstage.at[r], gout.at[0, r], out_sem.at[0])
        copy.start()
        outs.append(copy)
    for copy in outs:
        copy.wait()


def body(tokens, expert_ids, route_weights, out_grad, w_gate_up, w_down, second_moment):
    groups = lax.axis_size("narrow")
    wides = lax.axis_size("wide")
    count, width = tokens.shape
    cap = 3 * count // (2 * groups)
    slot = -(-cap // 16) * 16
    columns = w_gate_up.shape[2]
    units = w_down.shape[1]
    half = groups // 2
    all_rows = groups * 2 * slot
    last_rows = half * 2 * slot
    relayed = wides % 2 == 0 and wides >= 4
    chunks = len(FIRST_X) + half + half - 1 + (half - 1) * len(DIAGONAL_X) + half * len(LATE_D)
    dma = pltpu.SemaphoreType.DMA
    any_spec = pl.BlockSpec(memory_space=pl.ANY)
    vmem_spec = pl.BlockSpec(memory_space=pltpu.VMEM)
    held = pl.pallas_call(
        functools.partial(kernel, groups, wides, slot, relayed),
        out_shape=(
            pltpu.VMEM((width, columns), f32),
            pltpu.VMEM((width, last_rows), bf16),
            pltpu.VMEM((last_rows, columns), bf16),
            pltpu.VMEM((units, width), bf16),
        ),
        in_specs=[any_spec] * 7,
        out_specs=(vmem_spec,) * 4,
        scratch_shapes=[
            pltpu.VMEM((1, count), jnp.int32),
            pltpu.VMEM((1, count), f32),
            pltpu.VMEM((count, width), bf16),
            pltpu.VMEM((count, width), bf16),
            pltpu.VMEM((width, columns), bf16),
            pltpu.VMEM((units, width), bf16),
            pltpu.VMEM((units, width), bf16),
            pltpu.VMEM((groups - 1, slot, width), bf16),
            pltpu.VMEM((groups - 1, slot, width), bf16),
            pltpu.VMEM((all_rows, width), bf16),
            pltpu.VMEM((all_rows, width), bf16),
            pltpu.VMEM((slot, width), bf16),
            pltpu.VMEM((last_rows, columns), bf16),
            pltpu.VMEM((all_rows, units), bf16),
            pltpu.VMEM((units, width), f32),
            pltpu.VMEM((units, width), f32),
            pltpu.VMEM((units, width), f32),
            pltpu.VMEM((width, units), bf16),
            dma((6 + len(PACK),)), dma((1,)), dma((chunks,)), dma((max(LENDS, 1),)),
            dma((3 + len(LATE_D),)), pltpu.SemaphoreType.REGULAR, pltpu.SemaphoreType.REGULAR,
        ],
        compiler_params=pltpu.CompilerParams(
            collective_id=0, has_side_effects=True, vmem_limit_bytes=LIMIT
        ),
    )(
        *(
            pltpu.with_memory_space_constraint(value, pltpu.HBM)
            for value in (
                expert_ids.reshape(1, count), route_weights.reshape(1, count),
                tokens, out_grad, w_gate_up, w_down, second_moment,
            )
        ),
    )
    return pl.pallas_call(
        final_kernel,
        out_shape=(
            jax.ShapeDtypeStruct((1, width, columns), bf16),
            jax.ShapeDtypeStruct((1, units, width), bf16),
        ),
        in_specs=[vmem_spec] * 4,
        out_specs=(any_spec, any_spec),
        scratch_shapes=[pltpu.VMEM((width, columns), bf16), dma((1,))],
        compiler_params=pltpu.CompilerParams(vmem_limit_bytes=LIMIT),
    )(*held)


def solution(mesh):
    placed = (
        P(("wide", "narrow"), None),
        P(("wide", "narrow")),
        P(("wide", "narrow")),
        P(("wide", "narrow"), None),
        P(("wide", "narrow"), None, None),
        P(("wide", "narrow"), None, None),
        P(("wide", "narrow"), None, None),
    )
    return jax.shard_map(
        body,
        mesh=mesh,
        in_specs=placed,
        out_specs=(P(("wide", "narrow"), None, None), P(("wide", "narrow"), None, None)),
        check_vma=False,
    )
```

```python
import functools

import jax
import jax.numpy as jnp
from jax import lax
from jax.experimental import pallas as pl
from jax.experimental.pallas import tpu as pltpu
from jax.sharding import PartitionSpec as P

second_correction = 1.0 - 0.95**10
bf16 = jnp.bfloat16
f32 = jnp.float32
LIMIT = 32 * 1024 * 1024


def mm(a, b, dims):
    return lax.dot_general(a, b, (dims, ((), ())), preferred_element_type=f32)


LENDS = 2
AHEAD = 2
TURN = 1
PACK = (2, 3, 3)
FIRST_X = (2, 3, 3)
EARLY_D = (5, 3)
DIAGONAL_X = (4, 4)
LATE_D = (3, 2, 2, 1)


def spans(width, weights):
    unit = width // sum(weights)
    out, at = [], 0
    for weight in weights:
        out.append((at * unit, weight * unit))
        at += weight
    return out


def kernel(
    groups, wides, slot, relayed,
    ids_hbm, rw_hbm, tok_hbm, og_hbm, wgu_hbm, wdn_hbm, sm_hbm,
    acc_p, turned, pre_last, ustage,
    ids, rw, tok, og, wgu, wdn, sm, px, pd, rx, rd, lent, pre, hid, acc_d, moment, decay, turned_wdn,
    in_sem, sent_sem, recv_sem, lent_sem, frecv_sem, ready_sem, pair_sem,
):
    half = groups // 2
    width = tok.shape[1]
    hidden_units = wdn.shape[0]
    wide = lax.axis_index("wide")
    narrow = lax.axis_index("narrow")
    home = narrow // 2
    parity = lax.rem(narrow, 2)

    def along(step):
        return lax.rem(wide + wides + step, wides)

    def device(w, n):
        return {"wide": w, "narrow": n}

    def peer(j, other=0):
        return 2 * lax.rem(home + j, half) + lax.rem(parity + other, 2)

    def crossed(step, j):
        same = jnp.logical_and(along(step) == 0, lax.rem(home + j, half) == 0)
        return jnp.where(same, 0, 1)

    def target(step, j, a):
        return device(along(step), peer(j, crossed(step, j) if a else 0))

    odd = lax.rem(wide, 2) == 1
    even = jnp.logical_not(odd)
    sibling = device(wide, 2 * home + 1 - parity)
    leads = parity != crossed(0, 0)

    order = [(0, 0), (1, 0)] + [(0, j) for j in range(2, half)]
    order += [(0, 1)] + [(1, j) for j in range(1, half)]
    early = list(range(half))
    late = list(range(half, groups))
    direct = 1
    diagonal = [b for b in late if order[b][0]]
    beside = [b for b in range(1, groups) if not order[b][0]]

    pieces = spans(width, PACK)
    loads = {}

    def load(name, src, dst, i):
        loads[name] = pltpu.make_async_copy(src, dst, in_sem.at[i])

    load("ids", ids_hbm, ids, 0)
    for n, piece in enumerate(pieces):
        load(n, tok_hbm.at[:, pl.ds(*piece)], tok.at[:, pl.ds(*piece)], 1 if n == 0 else 4)
    load("rw", rw_hbm, rw, 0)
    load("og", og_hbm, og, 2)
    for copy in loads.values():
        copy.start()
    load("wgu", wgu_hbm.at[0], wgu, 3)
    load("wdn", wdn_hbm.at[0], wdn, 3)
    load("sm", sm_hbm.at[0], sm, 3)

    barrier = pltpu.get_barrier_semaphore()

    def signal(sem, partner):
        pl.semaphore_signal(sem, inc=1, device_id=partner, device_id_type=pl.DeviceIdType.MESH)

    signal(barrier, device(along(-1), narrow))
    for j in range(1, half):
        signal(barrier, device(wide, peer(j)))
    signal(barrier, sibling)
    if relayed:

        @pl.when(even)
        def _():
            signal(barrier, device(along(1), narrow))

    both = acc_d.at[pl.ds(0, 2), pl.ds(0, tok.shape[0])]
    pltpu.make_async_copy(both, both, in_sem.at[0]).wait()
    count = tok.shape[0]
    labels = ids[...]
    pad_groups = max(8, groups)
    onehot = (lax.broadcasted_iota(jnp.int32, (pad_groups, count), 0) == labels).astype(f32)
    before = (
        lax.broadcasted_iota(jnp.int32, (count, count), 0)
        < lax.broadcasted_iota(jnp.int32, (count, count), 1)
    ).astype(f32)
    counted = mm(onehot.astype(bf16), before.astype(bf16), ((1,), (0,)))
    within = jnp.sum(counted * onehot, axis=0, keepdims=True).astype(jnp.int32)
    slots = lax.broadcasted_iota(jnp.int32, (slot, count), 0)

    def select_of(b):
        kind, j = order[b]
        value = kind * half + lax.rem(home + j, half)
        return jnp.logical_and(labels == value, slots == within)

    near = half
    far = jnp.logical_and(wide == wides - 1, home > 0)
    swapped = jnp.logical_and(wide == 0, home > 0)
    near_swapped = jnp.logical_and(wide == 0, lax.rem(home + 1, half) > 0)
    lent_swapped = jnp.logical_and(along(2) == 0, home > 0)

    def rows(b, h, swap):
        at = jnp.where(swap, direct + near - b, b) if b in (direct, near) else b
        start = (2 * at + h) * slot
        return pl.ds(start if isinstance(start, int) else pl.multiple_of(start, slot), slot)

    def remote(src, dst, s, r, dev):
        return pltpu.make_async_remote_copy(
            src_ref=src, dst_ref=dst, send_sem=s, recv_sem=r,
            device_id=dev, device_id_type=pl.DeviceIdType.MESH,
        )

    index, parts, used = {}, {}, 0
    for b in range(1, groups):
        widths = (DIAGONAL_X if b in diagonal else FIRST_X, EARLY_D if b in early[2:] else LATE_D)
        for a in (0, 1):
            parts[b, a] = spans(width, widths[a])
            one = b in beside if a == 0 else b in early
            for c in range(len(parts[b, a])):
                index[b, a, c] = used if one else used + c
            used += 1 if one else len(parts[b, a])

    packed, received = (px, pd), (rx, rd)

    def cols_of(b, a, c):
        return pl.ds(*parts[b, a][c])

    def slot_of(b, a, c, swap):
        if a and b in (direct, near):
            return jnp.where(swap, index[direct + near - b, 1, c], index[b, 1, c])
        return index[b, a, c]

    def send(b, a, c):
        kind, j = order[b]
        cols, swap = cols_of(b, a, c), far if b == direct else near_swapped
        return remote(
            packed[a].at[b - 1, :, cols],
            received[a].at[rows(b, crossed(kind, j) if a else 0, swap), cols],
            sent_sem.at[0], recv_sem.at[slot_of(b, a, c, swap)], target(kind, j, a),
        )

    lends = LENDS if relayed else 0

    def lend(c):
        cols = cols_of(direct, 0, c)
        return remote(
            px.at[direct - 1, :, cols], lent.at[:, cols],
            sent_sem.at[0], lent_sem.at[c], device(along(-1), narrow),
        )

    def hand_on(c):
        cols = cols_of(direct, 0, c)
        return remote(
            lent.at[:, cols], rx.at[rows(direct, 0, lent_swapped), cols],
            sent_sem.at[0], recv_sem.at[index[direct, 0, c]], target(2, 0, 0),
        )

    def go_first(c):
        if relayed:

            @pl.when(odd)
            def _():
                lend(c).start()

            @pl.when(even)
            def _():
                send(direct, 0, c).start()
        else:
            send(direct, 0, c).start()

    def go_direct():
        for c in range(len(parts[direct, 1])):
            send(direct, 1, c).start()

    def go_more():
        for c in range(lends, len(FIRST_X)):
            send(direct, 0, c).start()

    held_back = jnp.logical_and(odd, wide != wides - 1) if relayed else wide < 0

    def go_rest():
        pl.when(held_back)(go_more)
        pl.when(jnp.logical_not(far))(go_direct)
        for a in (0, 1):
            for b in diagonal:
                for c in range(len(parts[b, a])):
                    send(b, a, c).start()

    first_columns = sum(FIRST_X[:lends]) * width // sum(FIRST_X)

    final = len(LATE_D)

    def heard(b, a):
        return crossed(0, 0) if a and b else 0

    def forward(b, a, cols, which):
        h = heard(b, a)
        return remote(
            received[a].at[rows(b, h, swapped), cols],
            received[a].at[rows(b, 1 - h, swapped), cols],
            sent_sem.at[0], frecv_sem.at[which], sibling,
        )

    def arrived(part, sem):
        return remote(part, part, sent_sem.at[0], sem, sibling)

    def settle(which, a, blocks, cols=slice(None)):
        arrived(received[a].at[pl.ds(0, blocks * slot), cols], frecv_sem.at[which]).wait_recv()

    selects = [select_of(b) for b in range(groups)]
    chosen = jnp.concatenate([s.astype(f32) for s in selects], axis=0).astype(bf16)

    def store(a, cols, block):
        for b in range(groups):
            piece = block[b * slot : (b + 1) * slot]
            if b:
                packed[a][b - 1, :, cols] = piece
            else:
                received[a][rows(0, 0, swapped), cols] = piece

    for n, (start, size) in enumerate(pieces):
        if n < 2:
            late_cols = pl.ds(pieces[n][0], (width if n else pieces[1][0]) - pieces[n][0])
            part = tok.at[:, late_cols]
            pltpu.make_async_copy(part, part, in_sem.at[4 if n else 1]).wait()
        cols = pl.ds(start, size)
        store(0, cols, mm(chosen, tok[:, cols], ((1,), (0,))).astype(bf16))
        if n == 0:
            entered = 1 + half - 1 + 1
            if relayed:

                @pl.when(odd)
                def _():
                    pl.semaphore_wait(barrier, entered + 1)

                @pl.when(even)
                def _():
                    pl.semaphore_wait(barrier, entered)
            else:
                pl.semaphore_wait(barrier, entered)
        for c, (at, extent) in enumerate(spans(width, FIRST_X)):
            if at + extent == start + size:
                if c < lends:
                    go_first(c)
                for b in beside:
                    send(b, 0, c).start()
        if n == 0:
            for j in range(1, half):
                signal(ready_sem, device(wide, peer(j)))
    pl.when(jnp.logical_not(held_back))(go_more)
    for name in ("wgu", "wdn", "sm"):
        loads[name].start()
    loads["og"].wait()
    weights = rw[...]
    weight = jnp.concatenate(
        [jnp.sum(jnp.where(s, weights, 0.0), axis=1, keepdims=True) for s in selects], axis=0
    )
    for start, size in spans(width, PACK):
        cols = pl.ds(start, size)
        placed = mm(chosen, og[:, cols], ((1,), (0,)))
        store(1, cols, (weight * placed).astype(bf16))
    if half > 1:
        pl.semaphore_wait(ready_sem, half - 1)
    signal(pair_sem, sibling)
    pl.semaphore_wait(pair_sem, 1)
    for b in beside:
        for c in range(len(parts[b, 1])):
            send(b, 1, c).start()
    if relayed:
        pl.when(jnp.logical_not(held_back))(go_rest)
    else:
        go_rest()
    for a in (0, 1):
        forward(0, a, slice(None), a).start()
    if relayed:

        @pl.when(even)
        def _():
            for c in range(lends):
                lend(c).wait_recv()
                hand_on(c).start()

    def project(r):
        projected = mm(rx[r, :], wgu[...], ((1,), (0,)))
        gate_pre = projected[:, :hidden_units]
        up_pre = projected[:, hidden_units:]
        logistic = jax.nn.sigmoid(gate_pre)
        swished = gate_pre * logistic
        hid[r, :] = (swished * up_pre).astype(bf16)
        return up_pre * logistic * (1.0 + gate_pre * (1.0 - logistic)), swished

    def finish(target, r, hidden_grad, factors):
        target[r, :] = jnp.concatenate(
            [hidden_grad * factors[0], hidden_grad * factors[1]], axis=1
        ).astype(bf16)

    def take(b, a, c, which):
        cols = cols_of(b, a, c)
        i = index[near if b == direct and a and which > 2 else b, a, c]
        arrived(received[a].at[rows(b, heard(b, a), swapped), cols], recv_sem.at[i]).wait_recv()
        forward(b, a, cols, which).start()

    def take_whole(b, a, which):
        i = index[direct if b == near and a else b, a, 0]
        arrived(received[a].at[rows(b, heard(b, a), swapped)], recv_sem.at[i]).wait_recv()
        forward(b, a, slice(None), which).start()

    for c in range(len(FIRST_X)):
        take(direct, 0, c, 0)
        if relayed and c < 2:
            pl.when(jnp.logical_and(held_back, parity == c))(go_rest)
    for b in beside:
        take_whole(b, 0, 0)
    settle(0, 0, half + 1)
    pl.when(far)(go_direct)
    pair = 2 * slot
    first, last = pl.ds(0, half * pair), pl.ds(half * pair, half * pair)
    soon, rest_rows = pl.ds(0, (half + 1) * pair), pl.ds((half + 1) * pair, (half - 1) * pair)
    pltpu.make_async_copy(acc_p, acc_p, in_sem.at[3]).wait()
    factors_soon = project(soon)
    factors_first = [factor[: half * pair] for factor in factors_soon]
    factors = [factor[half * pair :] for factor in factors_soon]
    for b in early[2:]:
        take_whole(b, 1, 1)

    @pl.when(jnp.logical_not(swapped))
    def _():
        take_whole(direct, 1, 1)

    @pl.when(swapped)
    def _():
        take_whole(near, 1, 1)

    moment[...] = (0.95 / second_correction) * sm[...].astype(f32)
    decay[...] = 0.1 * wdn[...].astype(f32)
    turned_wdn[...] = wdn[...].T
    settle(1, 1, half)
    finish(pre, first, mm(rd[first, :], wdn[...], ((1,), (1,))), factors_first)
    for i in range(width // 256):
        cols = pl.ds(i * 256, 256)
        acc_p[cols, :] = mm(rx[first, cols], pre[first, :], ((0,), (0,)))
        acc_d[:, cols] = mm(hid[first, :], rd[first, cols], ((0,), (0,)))
    for b in diagonal:
        for c in range(len(DIAGONAL_X)):
            take(b, 0, c, 2)

    def relay(c):
        for b in diagonal:
            take(b, 1, c, 3 + c)

        @pl.when(jnp.logical_not(swapped))
        def _():
            take(near, 1, c, 3 + c)

        @pl.when(swapped)
        def _():
            take(direct, 1, c, 3 + c)

    @pl.when(leads)
    def _():
        for c in range(final - 1):
            relay(c)

    settle(2, 0, half - 1)
    if half > 1:
        factors = [
            jnp.concatenate(both, axis=0) for both in zip(factors, project(rest_rows), strict=True)
        ]
    turned_hid = hid[last, :].T

    @pl.when(leads)
    def _():
        relay(final - 1)

    hidden_grad = jnp.zeros((half * 2 * slot, hidden_units), f32)
    late_d = spans(width, LATE_D)

    def add(c):
        cols = pl.ds(*late_d[c])
        return hidden_grad + mm(rd[last, cols], turned_wdn[cols, :], ((1,), (0,)))

    def update(c):
        cols = pl.ds(*late_d[c])
        total = acc_d[:, cols] + mm(turned_hid, rd[last, cols], ((1,), (0,)))
        second = moment[:, cols] + (0.05 / second_correction) * total * total
        root = second * lax.rsqrt(second)
        ustage[:, cols] = (total / (root + 1e-08) + decay[:, cols]).astype(bf16)

    follows = jnp.logical_not(leads)
    for c in range(AHEAD):
        pl.when(follows)(lambda c=c: relay(c))
    for c in range(final):
        if c + AHEAD < final:
            pl.when(follows)(lambda c=c: relay(c + AHEAD))

        settle(3 + c, 1, half, pl.ds(*late_d[c]))
        hidden_grad = add(c)
        if c + 1 == final:
            finish(pre_last, slice(None), hidden_grad, factors)
        update(c)
        if c == TURN:
            turned[...] = rx[last, :].T

    def sent(part):
        arrived(part, recv_sem.at[0]).wait_send()

    sent(px)
    sent(pd)
    sent(rx.at[pl.ds(0, groups * slot)])
    sent(rd.at[pl.ds(0, groups * slot)])
    if relayed:
        pl.when(even)(lambda: sent(lent.at[:, pl.ds(0, first_columns)]))


def final_kernel(acc_p, turned, pre_last, update, gout, uout, gstage, out_sem):
    tiles = acc_p.shape[0] // 256
    outs = [pltpu.make_async_copy(update, uout.at[0], out_sem.at[0])]
    outs[0].start()
    for i in range(tiles):
        r = pl.ds(i * 256, 256)
        gstage[r, :] = (acc_p[r, :] + mm(turned[r, :], pre_last[...], ((1,), (0,)))).astype(bf16)
        copy = pltpu.make_async_copy(gstage.at[r], gout.at[0, r], out_sem.at[0])
        copy.start()
        outs.append(copy)
    for copy in outs:
        copy.wait()


def body(tokens, expert_ids, route_weights, out_grad, w_gate_up, w_down, second_moment):
    groups = lax.axis_size("narrow")
    wides = lax.axis_size("wide")
    count, width = tokens.shape
    cap = 3 * count // (2 * groups)
    slot = -(-cap // 16) * 16
    columns = w_gate_up.shape[2]
    units = w_down.shape[1]
    half = groups // 2
    all_rows = groups * 2 * slot
    last_rows = half * 2 * slot
    relayed = wides % 2 == 0 and wides >= 4
    chunks = len(FIRST_X) + half + half - 1 + (half - 1) * len(DIAGONAL_X) + half * len(LATE_D)
    dma = pltpu.SemaphoreType.DMA
    any_spec = pl.BlockSpec(memory_space=pl.ANY)
    vmem_spec = pl.BlockSpec(memory_space=pltpu.VMEM)
    held = pl.pallas_call(
        functools.partial(kernel, groups, wides, slot, relayed),
        out_shape=(
            pltpu.VMEM((width, columns), f32),
            pltpu.VMEM((width, last_rows), bf16),
            pltpu.VMEM((last_rows, columns), bf16),
            pltpu.VMEM((units, width), bf16),
        ),
        in_specs=[any_spec] * 7,
        out_specs=(vmem_spec,) * 4,
        scratch_shapes=[
            pltpu.VMEM((1, count), jnp.int32),
            pltpu.VMEM((1, count), f32),
            pltpu.VMEM((count, width), bf16),
            pltpu.VMEM((count, width), bf16),
            pltpu.VMEM((width, columns), bf16),
            pltpu.VMEM((units, width), bf16),
            pltpu.VMEM((units, width), bf16),
            pltpu.VMEM((groups - 1, slot, width), bf16),
            pltpu.VMEM((groups - 1, slot, width), bf16),
            pltpu.VMEM((all_rows, width), bf16),
            pltpu.VMEM((all_rows, width), bf16),
            pltpu.VMEM((slot, width), bf16),
            pltpu.VMEM((last_rows, columns), bf16),
            pltpu.VMEM((all_rows, units), bf16),
            pltpu.VMEM((units, width), f32),
            pltpu.VMEM((units, width), f32),
            pltpu.VMEM((units, width), f32),
            pltpu.VMEM((width, units), bf16),
            dma((5,)), dma((1,)), dma((chunks,)), dma((LENDS,)),
            dma((3 + len(LATE_D),)), pltpu.SemaphoreType.REGULAR, pltpu.SemaphoreType.REGULAR,
        ],
        compiler_params=pltpu.CompilerParams(
            collective_id=0, has_side_effects=True, vmem_limit_bytes=LIMIT
        ),
    )(
        *(
            pltpu.with_memory_space_constraint(value, pltpu.HBM)
            for value in (
                expert_ids.reshape(1, count), route_weights.reshape(1, count),
                tokens, out_grad, w_gate_up, w_down, second_moment,
            )
        ),
    )
    return pl.pallas_call(
        final_kernel,
        out_shape=(
            jax.ShapeDtypeStruct((1, width, columns), bf16),
            jax.ShapeDtypeStruct((1, units, width), bf16),
        ),
        in_specs=[vmem_spec] * 4,
        out_specs=(any_spec, any_spec),
        scratch_shapes=[pltpu.VMEM((width, columns), bf16), dma((1,))],
        compiler_params=pltpu.CompilerParams(vmem_limit_bytes=LIMIT),
    )(*held)


def solution(mesh):
    placed = (
        P(("wide", "narrow"), None),
        P(("wide", "narrow")),
        P(("wide", "narrow")),
        P(("wide", "narrow"), None),
        P(("wide", "narrow"), None, None),
        P(("wide", "narrow"), None, None),
        P(("wide", "narrow"), None, None),
    )
    return jax.shard_map(
        body,
        mesh=mesh,
        in_specs=placed,
        out_specs=(P(("wide", "narrow"), None, None), P(("wide", "narrow"), None, None)),
        check_vma=False,
    )
```
